128 devices in a mesh: req: 32 (over x, z, core), tp: 4 (over y).
Axes of the slice: x: 4, y: 4, z: 4, core: 2. Of those that a mesh axis runs over, the one named last changes fastest.
Arguments:
- hidden_states: bfloat16 [8192, 2048], P('req'), may hold values from -30 to 30
- norm_gain: float32 [2048], replicated, may hold values from 0.5 to 1.5
- head: bfloat16 [2048, 98304], P(None, ('req', 'tp')), may hold values from -1 to 1
- target_ids: int32 [8192], P('req'), may hold values from 0 to 98303
- lengths: int32 [32], P('req'), may hold values from 32 to 256, as said below
Outputs:
- token_logprob: float32 [8192], P('req')
- token_entropy: float32 [8192], P('req')
- seq_mean_logprob: float32 [32], P('req')
- seq_top_logit: float32 [32], P('req')
The draws below stay inside these ranges and needn't reach their ends.
Inputs may be any that keep to these rules, and one draw needn't show every extreme that they name: `lengths`: each completion has at least 32 and at most 256 live slots; some completion has exactly 256.
All inputs are finite; a program needn't handle non-finite values.
Results may differ from the reference program's by a relative error of at most 0.0018.
Values may be sent and summed in bfloat16 or wider, within the bound.
A program may use at most 128 MiB of HBM per device.

```python
import math
import jax
import jax.numpy as jnp
import numpy as np
from jax import lax

D = 2048
LMAX = 256
LMIN = 32
NSEQ = 32
TOKENS = 8192
VOCAB = 98304


def draw_hidden_states(key, part):
    base = jax.random.normal(jax.random.fold_in(key, 1), (TOKENS, D), jnp.float32)
    return jnp.clip(base, -30.0, 30.0).astype(jnp.bfloat16)


def draw_head(key, part):
    root = jnp.sqrt(jnp.float32(D))
    noise = jax.random.normal(jax.random.fold_in(key, 3), (D, VOCAB), jnp.float32) * (1.6 / root)
    centers = jax.random.normal(jax.random.fold_in(key, 9), (D, 16), jnp.float32) * (1.2 / root)
    member = jax.random.randint(jax.random.fold_in(key, 10), (VOCAB,), 0, 16, dtype=jnp.int32)
    weights = noise + centers[:, member]
    return jnp.clip(weights, -1.0, 1.0).astype(jnp.bfloat16)


def draw_lengths(key, part):
    lens = jax.random.randint(jax.random.fold_in(key, 5), (NSEQ,), LMIN, LMAX + 1, dtype=jnp.int32)
    where_max = jax.random.randint(jax.random.fold_in(key, 6), (), 0, NSEQ, dtype=jnp.int32)
    return jnp.where(jnp.arange(NSEQ, dtype=jnp.int32) == where_max, jnp.int32(LMAX), lens)


def set_ends(values, stream_key, smallest, largest):
    longest = values.shape.index(max(values.shape))
    spots = []
    for shift in (0, 1):
        where = [jax.random.randint(jax.random.fold_in(stream_key, axis), (), 0, length) for axis, length in enumerate(values.shape)]
        where[longest] = (where[longest] + shift) % values.shape[longest]
        spots.append(tuple(where))
    return values.at[spots[0]].set(smallest).at[spots[1]].set(largest)


def skewed_wide(key, shape, number_of, lean):
    loads = [min(1 << octave, number_of + 1 - (1 << octave)) * (1 << 20) // math.isqrt((1 << octave) ** lean) + 1 for octave in range((number_of + 1).bit_length()) if 1 << octave <= number_of]
    width = 1 + sum(loads) // (1 << 30)
    table = np.cumsum(np.array([max(1, weight // width) for weight in loads]))
    pick = jax.random.randint(jax.random.fold_in(key, 1), shape, 0, int(table[len(loads) - 1]))
    start = jnp.left_shift(1, jnp.searchsorted(jnp.asarray(table, jnp.int32), pick, side="right").astype(jnp.int32))
    rank = start - 1 + jax.random.randint(jax.random.fold_in(key, 4), shape, 0, 1 << 30) % jnp.minimum(start, number_of + 1 - start)
    return jax.random.permutation(jax.random.fold_in(key, 2), number_of)[rank].astype(jnp.int32)


def setup_inputs(seed: int = 0) -> dict:
    key_of = jax.random.split(jax.random.key(seed), 6)
    return {
        "hidden_states": draw_hidden_states(jax.random.fold_in(key_of[5], 71), 0),
        "norm_gain": jnp.clip(1.0 + 0.1 * jax.random.normal(key_of[1], (D,), jnp.float32), 0.5, 1.5),
        "head": draw_head(jax.random.fold_in(key_of[5], 71), 0),
        "target_ids": set_ends(skewed_wide(key_of[3], (TOKENS,), VOCAB, 2), jax.random.fold_in(key_of[3], 3), 0, VOCAB - 1).astype(jnp.int32),
        "lengths": draw_lengths(jax.random.fold_in(key_of[5], 71), 0),
    }


def reference(hidden_states, norm_gain, head, target_ids, lengths):
    feats = hidden_states.astype(jnp.float32)
    scale = lax.rsqrt(lax.optimization_barrier(jnp.mean(feats * feats, axis=-1, keepdims=True)) + 1e-06)
    normed = (feats * scale * norm_gain.astype(jnp.float32)).astype(jnp.bfloat16)
    blocks = normed.reshape(NSEQ, LMAX, D)
    targets = target_ids.reshape(NSEQ, LMAX).astype(jnp.int32)

    def one_block(args):
        block, target = args
        logits = jnp.dot(block, head, preferred_element_type=jnp.float32)
        top = lax.optimization_barrier(jnp.max(logits, axis=-1))
        shifted = jnp.exp(logits - top[:, None])
        total = lax.optimization_barrier(jnp.sum(shifted, axis=-1))
        weighted = lax.optimization_barrier(jnp.sum(shifted * logits, axis=-1))
        picked = jnp.take_along_axis(logits, target[:, None], axis=1)[:, 0]
        return (top, total, weighted, picked)
    top, total, weighted, picked = lax.map(one_block, (blocks, targets))
    log_norm = top + jnp.log(total)
    slots = jnp.arange(LMAX, dtype=jnp.int32)
    live = slots[None, :] < lengths.astype(jnp.int32)[:, None]
    logprob = jnp.where(live, picked - log_norm, jnp.float32(0.0))
    entropy = jnp.where(live, log_norm - weighted / total, jnp.float32(0.0))
    mean_lp = lax.optimization_barrier(jnp.sum(logprob, axis=1)) / lengths.astype(jnp.float32)
    top_live = lax.optimization_barrier(jnp.max(jnp.where(live, top, jnp.float32(-1e+30)), axis=1))
    return (logprob.reshape(-1), entropy.reshape(-1), mean_lp, top_live)
```

```python
import jax
import jax.numpy as jnp
from jax import lax
from jax.sharding import PartitionSpec as P

CHUNKS = 4


def chunk_stats(block, target, matrix, vocab_ids):
    logits = jnp.dot(block, matrix, preferred_element_type=jnp.float32)
    top = jnp.max(logits, axis=-1)
    shifted = jnp.exp(logits - top[:, None])
    weight_sum = jnp.sum(shifted, axis=-1)
    weighted = jnp.sum(shifted * logits, axis=-1)
    hit = vocab_ids == target[:, None]
    picked = jnp.sum(jnp.where(hit, logits, 0.0), axis=-1)
    return jnp.stack([top, weight_sum, weighted, picked])


def merge(stats, axis):
    top = jnp.max(stats[:, 0], axis=axis)
    factor = jnp.exp(stats[:, 0] - jnp.expand_dims(top, axis))
    return (
        top,
        jnp.sum(stats[:, 1] * factor, axis=axis),
        jnp.sum(stats[:, 2] * factor, axis=axis),
        jnp.sum(stats[:, 3], axis=axis),
    )


def per_device(hidden_states, norm_gain, head, target_ids, lengths):
    feats = hidden_states.astype(jnp.float32)
    scale = lax.rsqrt(jnp.mean(feats * feats, axis=-1, keepdims=True) + 1e-06)
    normed = (feats * scale * norm_gain).astype(jnp.bfloat16)
    rows = hidden_states.shape[0]
    vdev = head.shape[1]
    n_req = lax.axis_size("req")
    n_tp = lax.axis_size("tp")
    vbase = (lax.axis_index("req") * n_tp + lax.axis_index("tp")) * vdev
    own_vocab = lax.broadcasted_iota(jnp.int32, (1, vdev), 1) + vbase
    step = rows // CHUNKS
    digits = jnp.concatenate([target_ids % 64, (target_ids // 64) % 64, target_ids // 4096])
    extra = jnp.zeros((16, normed.shape[1]), jnp.bfloat16)
    extra = extra.at[0, : 3 * rows].set(digits.astype(jnp.bfloat16))
    parts = []
    targets = None
    for c in range(CHUNKS):
        piece = normed[c * step:(c + 1) * step]
        if c == 0:
            piece = jnp.concatenate([piece, extra], axis=0)
        block = lax.all_gather(piece, "req", axis=0, tiled=False)
        if c == 0:
            code = block[:, step, : 3 * rows].astype(jnp.int32).reshape(n_req, 3, rows)
            targets = code[:, 0] + code[:, 1] * 64 + code[:, 2] * 4096
            block = block[:, :step]
        target = targets[:, c * step:(c + 1) * step].reshape(-1)
        st = chunk_stats(block.reshape(-1, block.shape[2]), target, head, own_vocab)
        parts.append(st.reshape(4, n_req, step))
    stats = jnp.concatenate(parts, axis=2)
    arrived = lax.all_to_all(stats, "req", split_axis=1, concat_axis=1, tiled=True)
    own = merge(jnp.moveaxis(arrived, 1, 0), axis=0)
    own = jnp.stack(own)
    everyone = lax.all_gather(own, "tp", axis=0)
    top, weight_sum, weighted, picked = merge(everyone, axis=0)
    log_norm = top + jnp.log(weight_sum)
    live = jnp.arange(rows, dtype=jnp.int32) < lengths[0]
    logprob = jnp.where(live, picked - log_norm, jnp.float32(0.0))
    entropy = jnp.where(live, log_norm - weighted / weight_sum, jnp.float32(0.0))
    mean_lp = (jnp.sum(logprob) / lengths[0].astype(jnp.float32)).reshape(1)
    top_live = jnp.max(jnp.where(live, top, jnp.float32(-1e30))).reshape(1)
    return (logprob, entropy, mean_lp, top_live)


def solution(mesh):
    in_specs = (P("req", None), P(), P(None, ("req", "tp")), P("req"), P("req"))
    out_specs = (P("req"), P("req"), P("req"), P("req"))
    return jax.shard_map(
        per_device, mesh=mesh, in_specs=in_specs, out_specs=out_specs, check_vma=False
    )
```

```python
import jax
import jax.numpy as jnp
import numpy as np
from jax import lax
from jax.experimental import pallas as pl
from jax.experimental.pallas import tpu as pltpu
from jax.sharding import Mesh, PartitionSpec as P

MESH = pl.DeviceIdType.MESH
PAD = 16


def swap_kernel(src_ref, dst_ref, send_sem, recv_sem):
    chip = lax.axis_index("chip")
    other = 1 - lax.axis_index("core")
    tp = lax.axis_index("tp")
    barrier = pltpu.get_barrier_semaphore()
    pl.semaphore_signal(barrier, inc=1, device_id=(chip, other, tp), device_id_type=MESH)
    pl.semaphore_wait(barrier, 1)
    copy = pltpu.make_async_remote_copy(
        src_ref=src_ref,
        dst_ref=dst_ref,
        send_sem=send_sem,
        recv_sem=recv_sem,
        device_id=(chip, other, tp),
        device_id_type=MESH,
    )
    copy.start()
    copy.wait()


def swap_with_other_core(head):
    return pl.pallas_call(
        swap_kernel,
        out_shape=jax.ShapeDtypeStruct(head.shape, head.dtype),
        in_specs=[pl.BlockSpec(memory_space=pl.ANY)],
        out_specs=pl.BlockSpec(memory_space=pl.ANY),
        scratch_shapes=[pltpu.SemaphoreType.DMA, pltpu.SemaphoreType.DMA],
        compiler_params=pltpu.CompilerParams(collective_id=0, has_side_effects=True),
    )(head)


def chunk_stats(block, target, matrix, vocab_ids):
    logits = jnp.dot(block, matrix, preferred_element_type=jnp.float32)
    top = jnp.max(logits, axis=-1)
    shifted = jnp.exp(logits - top[:, None])
    weight_sum = jnp.sum(shifted, axis=-1)
    weighted = jnp.sum(shifted * logits, axis=-1)
    hit = vocab_ids == target[:, None]
    picked = jnp.sum(jnp.where(hit, logits, 0.0), axis=-1)
    return jnp.stack([top, weight_sum, weighted, picked])


def merge(stats, axis):
    top = jnp.max(stats[:, 0], axis=axis)
    factor = jnp.exp(stats[:, 0] - jnp.expand_dims(top, axis))
    return (
        top,
        jnp.sum(stats[:, 1] * factor, axis=axis),
        jnp.sum(stats[:, 2] * factor, axis=axis),
        jnp.sum(stats[:, 3], axis=axis),
    )


def per_device(hidden_states, norm_gain, head, target_ids, lengths):
    feats = hidden_states.astype(jnp.float32)
    scale = lax.rsqrt(jnp.mean(feats * feats, axis=-1, keepdims=True) + 1e-06)
    normed = (feats * scale * norm_gain).astype(jnp.bfloat16)
    rows = hidden_states.shape[0]
    vdev = head.shape[1]
    n_chip = lax.axis_size("chip")
    n_tp = lax.axis_size("tp")
    chip = lax.axis_index("chip")
    core = lax.axis_index("core")
    tp = lax.axis_index("tp")
    digits = jnp.concatenate([target_ids % 64, (target_ids // 64) % 64, target_ids // 4096])
    extra = jnp.zeros((PAD, normed.shape[1]), jnp.bfloat16)
    extra = extra.at[0, : 3 * rows].set(digits.astype(jnp.bfloat16))
    piece = jnp.concatenate([normed, extra], axis=0)
    other_head = swap_with_other_core(head)
    block = lax.all_gather(piece, "chip", axis=0, tiled=False)
    code = block[:, rows, : 3 * rows].astype(jnp.int32).reshape(n_chip, 3, rows)
    targets = code[:, 0] + code[:, 1] * 64 + code[:, 2] * 4096
    targets = jnp.pad(targets, ((0, 0), (0, PAD)), constant_values=-1).reshape(-1)
    flat = block.reshape(-1, block.shape[2])
    columns = lax.broadcasted_iota(jnp.int32, (1, vdev), 1)
    own_base = ((chip * 2 + core) * n_tp + tp) * vdev
    other_base = ((chip * 2 + 1 - core) * n_tp + tp) * vdev
    s_own = chunk_stats(flat, targets, head, columns + own_base)
    s_other = chunk_stats(flat, targets, other_head, columns + other_base)
    first = jnp.where(core == 0, s_own, s_other)
    second = jnp.where(core == 0, s_other, s_own)
    pair = jnp.stack([first, second])
    stats = jnp.stack(merge(pair, axis=0)).reshape(4, n_chip, rows + PAD)[:, :, :rows]
    arrived = lax.all_to_all(stats, "chip", split_axis=1, concat_axis=1, tiled=True)
    own = jnp.stack(merge(jnp.moveaxis(arrived, 1, 0), axis=0))
    everyone = lax.all_gather(own, "tp", axis=0)
    top, weight_sum, weighted, picked = merge(everyone, axis=0)
    log_norm = top + jnp.log(weight_sum)
    live = jnp.arange(rows, dtype=jnp.int32) < lengths[0]
    logprob = jnp.where(live, picked - log_norm, jnp.float32(0.0))
    entropy = jnp.where(live, log_norm - weighted / weight_sum, jnp.float32(0.0))
    mean_lp = (jnp.sum(logprob) / lengths[0].astype(jnp.float32)).reshape(1)
    top_live = jnp.max(jnp.where(live, top, jnp.float32(-1e30))).reshape(1)
    return (logprob, entropy, mean_lp, top_live)


def solution(mesh):
    n_req, n_tp = mesh.devices.shape
    devices = np.asarray(mesh.devices).reshape(n_req // 2, 2, n_tp)
    fine = Mesh(devices, ("chip", "core", "tp"))
    rq = ("chip", "core")
    in_specs = (P(rq, None), P(), P(None, (*rq, "tp")), P(rq), P(rq))
    out_specs = (P(rq), P(rq), P(rq), P(rq))
    return jax.shard_map(
        per_device, mesh=fine, in_specs=in_specs, out_specs=out_specs, check_vma=False
    )
```

```python
import jax
import jax.numpy as jnp
import numpy as np
from jax import lax
from jax.experimental import pallas as pl
from jax.experimental.pallas import tpu as pltpu
from jax.sharding import Mesh, PartitionSpec as P

MESH = pl.DeviceIdType.MESH
EXTRA = 128


def swap_kernel(src_ref, dst_ref, send_sem, recv_sem):
    peer = (lax.axis_index("x"), lax.axis_index("z"), 1 - lax.axis_index("core"), lax.axis_index("tp"))
    barrier = pltpu.get_barrier_semaphore()
    pl.semaphore_signal(barrier, inc=1, device_id=peer, device_id_type=MESH)
    pl.semaphore_wait(barrier, 1)
    copy = pltpu.make_async_remote_copy(
        src_ref=src_ref,
        dst_ref=dst_ref,
        send_sem=send_sem,
        recv_sem=recv_sem,
        device_id=peer,
        device_id_type=MESH,
    )
    copy.start()
    copy.wait()


def swap_with_other_core(head):
    return pl.pallas_call(
        swap_kernel,
        out_shape=jax.ShapeDtypeStruct(head.shape, head.dtype),
        in_specs=[pl.BlockSpec(memory_space=pl.ANY)],
        out_specs=pl.BlockSpec(memory_space=pl.ANY),
        scratch_shapes=[pltpu.SemaphoreType.DMA, pltpu.SemaphoreType.DMA],
        compiler_params=pltpu.CompilerParams(collective_id=0, has_side_effects=True),
    )(head)


def slice_stats(block, target, matrix, vocab_ids):
    logits = jnp.dot(block, matrix, preferred_element_type=jnp.float32)
    top = jnp.max(logits, axis=-1)
    shifted = jnp.exp(logits - top[:, None])
    weight_sum = jnp.sum(shifted, axis=-1)
    weighted = jnp.sum(shifted * logits, axis=-1)
    hit = vocab_ids == target[:, None]
    picked = jnp.sum(jnp.where(hit, logits, 0.0), axis=-1)
    return jnp.stack([top, weight_sum, weighted, picked])


def merge(stats, axis):
    top = jnp.max(stats[:, 0], axis=axis)
    factor = jnp.exp(stats[:, 0] - jnp.expand_dims(top, axis))
    return (
        top,
        jnp.sum(stats[:, 1] * factor, axis=axis),
        jnp.sum(stats[:, 2] * factor, axis=axis),
        jnp.sum(stats[:, 3], axis=axis),
    )


def ring4(v, axis):
    up = [(i, (i + 1) % 4) for i in range(4)]
    down = [(i, (i - 1) % 4) for i in range(4)]
    from_minus = lax.ppermute(v, axis, perm=up)
    from_plus = lax.ppermute(v, axis, perm=down)
    h = v.shape[-2] // 2
    far_a = lax.ppermute(from_minus[..., :h, :], axis, perm=up)
    far_b = lax.ppermute(from_plus[..., h:, :], axis, perm=down)
    far = jnp.concatenate([far_a, far_b], axis=-2)
    return from_plus, far, from_minus


def per_device(hidden_states, norm_gain, head, target_ids, lengths):
    feats = hidden_states.astype(jnp.float32)
    scale = lax.rsqrt(jnp.mean(feats * feats, axis=-1, keepdims=True) + 1e-06)
    normed = (feats * scale * norm_gain).astype(jnp.bfloat16)
    rows, dim = normed.shape
    vdev = head.shape[1]
    n_tp = lax.axis_size("tp")
    xi = lax.axis_index("x")
    zi = lax.axis_index("z")
    core = lax.axis_index("core")
    tp = lax.axis_index("tp")
    n_z = lax.axis_size("z")
    chip = xi * n_z + zi
    digits = jnp.stack([target_ids % 64, (target_ids // 64) % 64, target_ids // 4096], axis=1)
    tail = jnp.zeros((rows, EXTRA), jnp.bfloat16).at[:, :3].set(digits.astype(jnp.bfloat16))
    piece = jnp.concatenate([normed, tail], axis=1)
    head_ext = jnp.concatenate([head, jnp.zeros((EXTRA, vdev), head.dtype)], axis=0)
    other_head = swap_with_other_core(head_ext)
    columns = lax.broadcasted_iota(jnp.int32, (1, vdev), 1)
    own_ids = columns + ((chip * 2 + core) * n_tp + tp) * vdev
    other_ids = columns + ((chip * 2 + 1 - core) * n_tp + tp) * vdev

    def stats_of(block):
        lead = block.shape[:-2]
        flat = block.reshape(-1, block.shape[-1])
        code = flat[:, dim:dim + 3].astype(jnp.int32)
        target = code[:, 0] + code[:, 1] * 64 + code[:, 2] * 4096
        s_own = slice_stats(flat, target, head_ext, own_ids)
        s_other = slice_stats(flat, target, other_head, other_ids)
        first = jnp.where(core == 0, s_own, s_other)
        second = jnp.where(core == 0, s_other, s_own)
        merged = jnp.stack(merge(jnp.stack([first, second]), axis=0))
        return merged.reshape(4, *lead, block.shape[-2])

    half = rows // 2
    results = {}
    for name, part, first_axis, second_axis in (("a", piece[:half], "x", "z"), ("b", piece[half:], "z", "x")):
        p1, p2, p3 = ring4(part, first_axis)
        line = jnp.stack([part, p1, p2, p3])
        s_line = stats_of(line)
        q1, q2, q3 = ring4(line, second_axis)
        s_rest = [stats_of(q) for q in (q1, q2, q3)]
        results[name] = jnp.stack([s_line] + s_rest, axis=1)
    s_a = results["a"]
    s_b = jnp.swapaxes(results["b"], 1, 2)
    rel = jnp.concatenate([s_a, s_b], axis=3)
    absolute = jnp.roll(jnp.roll(rel, zi, axis=1), xi, axis=2)
    by_chip = jnp.swapaxes(absolute, 1, 2).reshape(4, -1, rows)
    arrived = lax.all_to_all(by_chip, ("x", "z"), split_axis=1, concat_axis=1, tiled=True)
    own = jnp.stack(merge(jnp.moveaxis(arrived, 1, 0), axis=0))
    everyone = lax.all_gather(own, "tp", axis=0)
    top, weight_sum, weighted, picked = merge(everyone, axis=0)
    log_norm = top + jnp.log(weight_sum)
    live = jnp.arange(rows, dtype=jnp.int32) < lengths[0]
    logprob = jnp.where(live, picked - log_norm, jnp.float32(0.0))
    entropy = jnp.where(live, log_norm - weighted / weight_sum, jnp.float32(0.0))
    mean_lp = (jnp.sum(logprob) / lengths[0].astype(jnp.float32)).reshape(1)
    top_live = jnp.max(jnp.where(live, top, jnp.float32(-1e30))).reshape(1)
    return (logprob, entropy, mean_lp, top_live)


def solution(mesh):
    n_req, n_tp = mesh.devices.shape
    devices = np.asarray(mesh.devices).reshape(4, n_req // 8, 2, n_tp)
    fine = Mesh(devices, ("x", "z", "core", "tp"))
    rq = ("x", "z", "core")
    in_specs = (P(rq, None), P(), P(None, (*rq, "tp")), P(rq), P(rq))
    out_specs = (P(rq), P(rq), P(rq), P(rq))
    return jax.shard_map(
        per_device, mesh=fine, in_specs=in_specs, out_specs=out_specs, check_vma=False
    )
```

```python
import jax
import jax.numpy as jnp
import numpy as np
from jax import lax
from jax.experimental import pallas as pl
from jax.experimental.pallas import tpu as pltpu
from jax.sharding import Mesh, PartitionSpec as P

MESH = pl.DeviceIdType.MESH
EXTRA = 128


def swap_kernel(src_ref, dst_ref, send_sem, recv_sem):
    peer = (lax.axis_index("x"), lax.axis_index("z"), 1 - lax.axis_index("core"), lax.axis_index("tp"))
    barrier = pltpu.get_barrier_semaphore()
    pl.semaphore_signal(barrier, inc=1, device_id=peer, device_id_type=MESH)
    pl.semaphore_wait(barrier, 1)
    copy = pltpu.make_async_remote_copy(
        src_ref=src_ref,
        dst_ref=dst_ref,
        send_sem=send_sem,
        recv_sem=recv_sem,
        device_id=peer,
        device_id_type=MESH,
    )
    copy.start()
    copy.wait()


def swap_with_other_core(head):
    return pl.pallas_call(
        swap_kernel,
        out_shape=jax.ShapeDtypeStruct(head.shape, head.dtype),
        in_specs=[pl.BlockSpec(memory_space=pl.ANY)],
        out_specs=pl.BlockSpec(memory_space=pl.ANY),
        scratch_shapes=[pltpu.SemaphoreType.DMA, pltpu.SemaphoreType.DMA],
        compiler_params=pltpu.CompilerParams(collective_id=0, has_side_effects=True),
    )(head)


def slice_stats(block, target, matrix, vocab_ids):
    logits = jnp.dot(block, matrix, preferred_element_type=jnp.float32)
    top = jnp.max(logits, axis=-1)
    shifted = jnp.exp(logits - top[:, None])
    weight_sum = jnp.sum(shifted, axis=-1)
    weighted = jnp.sum(shifted * logits, axis=-1)
    hit = vocab_ids == target[:, None]
    picked = jnp.sum(jnp.where(hit, logits, 0.0), axis=-1)
    return jnp.stack([top, weight_sum, weighted, picked])


def merge(stats, axis):
    top = jnp.max(stats[:, 0], axis=axis)
    factor = jnp.exp(stats[:, 0] - jnp.expand_dims(top, axis))
    return (
        top,
        jnp.sum(stats[:, 1] * factor, axis=axis),
        jnp.sum(stats[:, 2] * factor, axis=axis),
        jnp.sum(stats[:, 3], axis=axis),
    )


def gather_kernel(piece_ref, out_ref, own_sem, send_sems, recv_sems):
    xi, zi = lax.axis_index("x"), lax.axis_index("z")
    core, tp = lax.axis_index("core"), lax.axis_index("tp")

    def dev(dx, dz):
        return (lax.rem(xi + dx, 4), lax.rem(zi + dz, 4), core, tp)

    barrier = pltpu.get_barrier_semaphore()
    for dx, dz in ((1, 0), (3, 0), (0, 1), (0, 3)):
        pl.semaphore_signal(barrier, inc=1, device_id=dev(dx, dz), device_id_type=MESH)
    pl.semaphore_wait(barrier, 4)
    own = pltpu.make_async_copy(piece_ref, out_ref.at[0, 0], own_sem)
    own.start()
    rows = piece_ref.shape[0]
    h, q = rows // 2, rows // 4
    count = [0]

    def send(src, dst, dx, dz):
        k = count[0]
        count[0] += 1
        cp = pltpu.make_async_remote_copy(
            src_ref=src,
            dst_ref=dst,
            send_sem=send_sems.at[k],
            recv_sem=recv_sems.at[k],
            device_id=dev(dx, dz),
            device_id_type=MESH,
        )
        cp.start()
        return cp

    def finish(cps):
        for cp in cps:
            cp.wait()

    finish([
        send(piece_ref.at[0:h], out_ref.at[0, 3, 0:h], 1, 0),
        send(piece_ref.at[0:h], out_ref.at[0, 1, 0:h], 3, 0),
        send(piece_ref.at[h:rows], out_ref.at[3, 0, h:rows], 0, 1),
        send(piece_ref.at[h:rows], out_ref.at[1, 0, h:rows], 0, 3),
    ])
    finish([
        send(out_ref.at[0, 3, 0:q], out_ref.at[0, 2, 0:q], 1, 0),
        send(out_ref.at[0, 1, q:h], out_ref.at[0, 2, q:h], 3, 0),
        send(out_ref.at[3, 0, h:h + q], out_ref.at[2, 0, h:h + q], 0, 1),
        send(out_ref.at[1, 0, h + q:rows], out_ref.at[2, 0, h + q:rows], 0, 3),
    ])
    own.wait()
    finish([
        send(out_ref.at[0, :, 0:h], out_ref.at[3, :, 0:h], 0, 1),
        send(out_ref.at[0, :, 0:h], out_ref.at[1, :, 0:h], 0, 3),
        send(out_ref.at[:, 0, h:rows], out_ref.at[:, 3, h:rows], 1, 0),
        send(out_ref.at[:, 0, h:rows], out_ref.at[:, 1, h:rows], 3, 0),
    ])
    finish([
        send(out_ref.at[3, :, 0:q], out_ref.at[2, :, 0:q], 0, 1),
        send(out_ref.at[1, :, q:h], out_ref.at[2, :, q:h], 0, 3),
        send(out_ref.at[:, 3, h:h + q], out_ref.at[:, 2, h:h + q], 1, 0),
        send(out_ref.at[:, 1, h + q:rows], out_ref.at[:, 2, h + q:rows], 3, 0),
    ])


def gather_plane(piece):
    rows, cols = piece.shape
    return pl.pallas_call(
        gather_kernel,
        out_shape=jax.ShapeDtypeStruct((4, 4, rows, cols), piece.dtype),
        in_specs=[pl.BlockSpec(memory_space=pl.ANY)],
        out_specs=pl.BlockSpec(memory_space=pl.ANY),
        scratch_shapes=[
            pltpu.SemaphoreType.DMA,
            pltpu.SemaphoreType.DMA((16,)),
            pltpu.SemaphoreType.DMA((16,)),
        ],
        compiler_params=pltpu.CompilerParams(collective_id=1, has_side_effects=True),
    )(piece)


def per_device(hidden_states, norm_gain, head, target_ids, lengths):
    feats = hidden_states.astype(jnp.float32)
    scale = lax.rsqrt(jnp.mean(feats * feats, axis=-1, keepdims=True) + 1e-06)
    normed = (feats * scale * norm_gain).astype(jnp.bfloat16)
    rows, dim = normed.shape
    vdev = head.shape[1]
    n_tp = lax.axis_size("tp")
    xi = lax.axis_index("x")
    zi = lax.axis_index("z")
    core = lax.axis_index("core")
    tp = lax.axis_index("tp")
    n_z = lax.axis_size("z")
    chip = xi * n_z + zi
    digits = jnp.stack([target_ids % 64, (target_ids // 64) % 64, target_ids // 4096], axis=1)
    tail = jnp.zeros((rows, EXTRA), jnp.bfloat16).at[:, :3].set(digits.astype(jnp.bfloat16))
    piece = jnp.concatenate([normed, tail], axis=1)
    head_ext = jnp.concatenate([head, jnp.zeros((EXTRA, vdev), head.dtype)], axis=0)
    other_head = swap_with_other_core(head_ext)
    columns = lax.broadcasted_iota(jnp.int32, (1, vdev), 1)
    own_ids = columns + ((chip * 2 + core) * n_tp + tp) * vdev
    other_ids = columns + ((chip * 2 + 1 - core) * n_tp + tp) * vdev

    def stats_of(block):
        lead = block.shape[:-2]
        flat = block.reshape(-1, block.shape[-1])
        code = flat[:, dim:dim + 3].astype(jnp.int32)
        target = code[:, 0] + code[:, 1] * 64 + code[:, 2] * 4096
        s_own = slice_stats(flat, target, head_ext, own_ids)
        s_other = slice_stats(flat, target, other_head, other_ids)
        first = jnp.where(core == 0, s_own, s_other)
        second = jnp.where(core == 0, s_other, s_own)
        merged = jnp.stack(merge(jnp.stack([first, second]), axis=0))
        return merged.reshape(4, *lead, block.shape[-2])

    gathered = gather_plane(piece)
    rel = stats_of(gathered.reshape(-1, gathered.shape[-1])).reshape(4, 4, 4, rows)
    absolute = jnp.roll(jnp.roll(rel, zi, axis=1), xi, axis=2)
    by_chip = jnp.swapaxes(absolute, 1, 2).reshape(4, -1, rows)
    arrived = lax.all_to_all(by_chip, ("x", "z"), split_axis=1, concat_axis=1, tiled=True)
    own = jnp.stack(merge(jnp.moveaxis(arrived, 1, 0), axis=0))
    everyone = lax.all_gather(own, "tp", axis=0)
    top, weight_sum, weighted, picked = merge(everyone, axis=0)
    log_norm = top + jnp.log(weight_sum)
    live = jnp.arange(rows, dtype=jnp.int32) < lengths[0]
    logprob = jnp.where(live, picked - log_norm, jnp.float32(0.0))
    entropy = jnp.where(live, log_norm - weighted / weight_sum, jnp.float32(0.0))
    mean_lp = (jnp.sum(logprob) / lengths[0].astype(jnp.float32)).reshape(1)
    top_live = jnp.max(jnp.where(live, top, jnp.float32(-1e30))).reshape(1)
    return (logprob, entropy, mean_lp, top_live)


def solution(mesh):
    n_req, n_tp = mesh.devices.shape
    devices = np.asarray(mesh.devices).reshape(4, n_req // 8, 2, n_tp)
    fine = Mesh(devices, ("x", "z", "core", "tp"))
    rq = ("x", "z", "core")
    in_specs = (P(rq, None), P(), P(None, (*rq, "tp")), P(rq), P(rq))
    out_specs = (P(rq), P(rq), P(rq), P(rq))
    return jax.shard_map(
        per_device, mesh=fine, in_specs=in_specs, out_specs=out_specs, check_vma=False
    )
```

```python
import jax
import jax.numpy as jnp
import numpy as np
from jax import lax
from jax.experimental import pallas as pl
from jax.experimental.pallas import tpu as pltpu
from jax.sharding import Mesh, PartitionSpec as P

MESH = pl.DeviceIdType.MESH
EXTRA = 128


def slice_stats(block, target, matrix, vocab_ids):
    logits = jnp.dot(block, matrix, preferred_element_type=jnp.float32)
    top = jnp.max(logits, axis=-1)
    shifted = jnp.exp(logits - top[:, None])
    weight_sum = jnp.sum(shifted, axis=-1)
    weighted = jnp.sum(shifted * logits, axis=-1)
    hit = vocab_ids == target[:, None]
    picked = jnp.sum(jnp.where(hit, logits, 0.0), axis=-1)
    return jnp.stack([top, weight_sum, weighted, picked])


def merge(stats, axis):
    top = jnp.max(stats[:, 0], axis=axis)
    factor = jnp.exp(stats[:, 0] - jnp.expand_dims(top, axis))
    return (
        top,
        jnp.sum(stats[:, 1] * factor, axis=axis),
        jnp.sum(stats[:, 2] * factor, axis=axis),
        jnp.sum(stats[:, 3], axis=axis),
    )


def gather_kernel(piece_ref, head_ref, out_ref, other_ref, own_sem, head_sems, send_sems, recv_sems):
    xi, zi = lax.axis_index("x"), lax.axis_index("z")
    core, tp = lax.axis_index("core"), lax.axis_index("tp")

    def dev(dx, dz):
        return (lax.rem(xi + dx, 4), lax.rem(zi + dz, 4), core, tp)

    partner = (xi, zi, 1 - core, tp)
    barrier = pltpu.get_barrier_semaphore()
    for dx, dz in ((1, 0), (3, 0), (0, 1), (0, 3)):
        pl.semaphore_signal(barrier, inc=1, device_id=dev(dx, dz), device_id_type=MESH)
    pl.semaphore_signal(barrier, inc=1, device_id=partner, device_id_type=MESH)
    pl.semaphore_wait(barrier, 5)
    swap = pltpu.make_async_remote_copy(
        src_ref=head_ref,
        dst_ref=other_ref,
        send_sem=head_sems.at[0],
        recv_sem=head_sems.at[1],
        device_id=partner,
        device_id_type=MESH,
    )
    swap.start()
    own = pltpu.make_async_copy(piece_ref, out_ref.at[0, 0], own_sem)
    own.start()
    rows = piece_ref.shape[0]
    h, q = rows // 2, rows // 4
    count = [0]

    def send(src, dst, dx, dz):
        k = count[0]
        count[0] += 1
        cp = pltpu.make_async_remote_copy(
            src_ref=src,
            dst_ref=dst,
            send_sem=send_sems.at[k],
            recv_sem=recv_sems.at[k],
            device_id=dev(dx, dz),
            device_id_type=MESH,
        )
        cp.start()
        return cp

    def finish(cps):
        for cp in cps:
            cp.wait()

    finish([
        send(piece_ref.at[0:h], out_ref.at[0, 3, 0:h], 1, 0),
        send(piece_ref.at[0:h], out_ref.at[0, 1, 0:h], 3, 0),
        send(piece_ref.at[h:rows], out_ref.at[3, 0, h:rows], 0, 1),
        send(piece_ref.at[h:rows], out_ref.at[1, 0, h:rows], 0, 3),
    ])
    finish([
        send(out_ref.at[0, 3, 0:q], out_ref.at[0, 2, 0:q], 1, 0),
        send(out_ref.at[0, 1, q:h], out_ref.at[0, 2, q:h], 3, 0),
        send(out_ref.at[3, 0, h:h + q], out_ref.at[2, 0, h:h + q], 0, 1),
        send(out_ref.at[1, 0, h + q:rows], out_ref.at[2, 0, h + q:rows], 0, 3),
    ])
    own.wait()
    finish([
        send(out_ref.at[0, :, 0:h], out_ref.at[3, :, 0:h], 0, 1),
        send(out_ref.at[0, :, 0:h], out_ref.at[1, :, 0:h], 0, 3),
        send(out_ref.at[:, 0, h:rows], out_ref.at[:, 3, h:rows], 1, 0),
        send(out_ref.at[:, 0, h:rows], out_ref.at[:, 1, h:rows], 3, 0),
    ])
    finish([
        send(out_ref.at[3, :, 0:q], out_ref.at[2, :, 0:q], 0, 1),
        send(out_ref.at[1, :, q:h], out_ref.at[2, :, q:h], 0, 3),
        send(out_ref.at[:, 3, h:h + q], out_ref.at[:, 2, h:h + q], 1, 0),
        send(out_ref.at[:, 1, h + q:rows], out_ref.at[:, 2, h + q:rows], 3, 0),
    ])
    swap.wait()


def gather_plane(piece, head):
    rows, cols = piece.shape
    return pl.pallas_call(
        gather_kernel,
        out_shape=(
            jax.ShapeDtypeStruct((4, 4, rows, cols), piece.dtype),
            jax.ShapeDtypeStruct(head.shape, head.dtype),
        ),
        in_specs=[pl.BlockSpec(memory_space=pl.ANY)] * 2,
        out_specs=(pl.BlockSpec(memory_space=pl.ANY), pl.BlockSpec(memory_space=pl.ANY)),
        scratch_shapes=[
            pltpu.SemaphoreType.DMA,
            pltpu.SemaphoreType.DMA((2,)),
            pltpu.SemaphoreType.DMA((16,)),
            pltpu.SemaphoreType.DMA((16,)),
        ],
        compiler_params=pltpu.CompilerParams(collective_id=1, has_side_effects=True),
    )(piece, head)


def plane_kernel(stats_ref, out_ref, own_sem, send_sems, recv_sems):
    xi, zi = lax.axis_index("x"), lax.axis_index("z")
    core, tp = lax.axis_index("core"), lax.axis_index("tp")
    offsets = [(dx, dz) for dz in range(4) for dx in range(4) if dx or dz]
    barrier = pltpu.get_barrier_semaphore()
    for dx, dz in offsets:
        peer = (lax.rem(xi + dx, 4), lax.rem(zi + dz, 4), core, tp)
        pl.semaphore_signal(barrier, inc=1, device_id=peer, device_id_type=MESH)
    pl.semaphore_wait(barrier, len(offsets))
    own = pltpu.make_async_copy(stats_ref.at[0, 0], out_ref.at[0, 0], own_sem)
    own.start()
    cps = []
    for k, (dx, dz) in enumerate(offsets):
        peer = (lax.rem(xi + dx, 4), lax.rem(zi + dz, 4), core, tp)
        cp = pltpu.make_async_remote_copy(
            src_ref=stats_ref.at[dz, dx],
            dst_ref=out_ref.at[(4 - dz) % 4, (4 - dx) % 4],
            send_sem=send_sems.at[k],
            recv_sem=recv_sems.at[k],
            device_id=peer,
            device_id_type=MESH,
        )
        cp.start()
        cps.append(cp)
    own.wait()
    for cp in cps:
        cp.wait()


def exchange_plane(stats):
    return pl.pallas_call(
        plane_kernel,
        out_shape=jax.ShapeDtypeStruct(stats.shape, stats.dtype),
        in_specs=[pl.BlockSpec(memory_space=pl.ANY)],
        out_specs=pl.BlockSpec(memory_space=pl.ANY),
        scratch_shapes=[
            pltpu.SemaphoreType.DMA,
            pltpu.SemaphoreType.DMA((15,)),
            pltpu.SemaphoreType.DMA((15,)),
        ],
        compiler_params=pltpu.CompilerParams(collective_id=2, has_side_effects=True),
    )(stats)


def tp_kernel(own_ref, out_ref, own_sem, send_sems, recv_sems):
    xi, zi = lax.axis_index("x"), lax.axis_index("z")
    core, tp = lax.axis_index("core"), lax.axis_index("tp")
    n = out_ref.shape[0]
    barrier = pltpu.get_barrier_semaphore()
    for d in range(1, n):
        peer = (xi, zi, core, lax.rem(tp + d, n))
        pl.semaphore_signal(barrier, inc=1, device_id=peer, device_id_type=MESH)
    pl.semaphore_wait(barrier, n - 1)
    own = pltpu.make_async_copy(own_ref, out_ref.at[tp], own_sem)
    own.start()
    cps = []
    for d in range(1, n):
        peer = (xi, zi, core, lax.rem(tp + d, n))
        cp = pltpu.make_async_remote_copy(
            src_ref=own_ref,
            dst_ref=out_ref.at[tp],
            send_sem=send_sems.at[d - 1],
            recv_sem=recv_sems.at[d - 1],
            device_id=peer,
            device_id_type=MESH,
        )
        cp.start()
        cps.append(cp)
    own.wait()
    for cp in cps:
        cp.wait()


def exchange_tp(own, n_tp):
    return pl.pallas_call(
        tp_kernel,
        out_shape=jax.ShapeDtypeStruct((n_tp, *own.shape), own.dtype),
        in_specs=[pl.BlockSpec(memory_space=pl.ANY)],
        out_specs=pl.BlockSpec(memory_space=pl.ANY),
        scratch_shapes=[
            pltpu.SemaphoreType.DMA,
            pltpu.SemaphoreType.DMA((n_tp - 1,)),
            pltpu.SemaphoreType.DMA((n_tp - 1,)),
        ],
        compiler_params=pltpu.CompilerParams(collective_id=3, has_side_effects=True),
    )(own)


def per_device(hidden_states, norm_gain, head, target_ids, lengths):
    feats = hidden_states.astype(jnp.float32)
    scale = lax.rsqrt(jnp.mean(feats * feats, axis=-1, keepdims=True) + 1e-06)
    normed = (feats * scale * norm_gain).astype(jnp.bfloat16)
    rows, dim = normed.shape
    vdev = head.shape[1]
    n_tp = lax.axis_size("tp")
    xi = lax.axis_index("x")
    zi = lax.axis_index("z")
    core = lax.axis_index("core")
    tp = lax.axis_index("tp")
    n_z = lax.axis_size("z")
    chip = xi * n_z + zi
    digits = jnp.stack([target_ids % 64, (target_ids // 64) % 64, target_ids // 4096], axis=1)
    tail = jnp.zeros((rows, EXTRA), jnp.bfloat16).at[:, :3].set(digits.astype(jnp.bfloat16))
    piece = jnp.concatenate([normed, tail], axis=1)
    head_ext = jnp.concatenate([head, jnp.zeros((EXTRA, vdev), head.dtype)], axis=0)
    columns = lax.broadcasted_iota(jnp.int32, (1, vdev), 1)
    own_ids = columns + ((chip * 2 + core) * n_tp + tp) * vdev
    other_ids = columns + ((chip * 2 + 1 - core) * n_tp + tp) * vdev

    def stats_of(block):
        lead = block.shape[:-2]
        flat = block.reshape(-1, block.shape[-1])
        code = flat[:, dim:dim + 3].astype(jnp.int32)
        target = code[:, 0] + code[:, 1] * 64 + code[:, 2] * 4096
        s_own = slice_stats(flat, target, head_ext, own_ids)
        s_other = slice_stats(flat, target, other_head, other_ids)
        first = jnp.where(core == 0, s_own, s_other)
        second = jnp.where(core == 0, s_other, s_own)
        merged = jnp.stack(merge(jnp.stack([first, second]), axis=0))
        return merged.reshape(4, *lead, block.shape[-2])

    gathered, other_head = gather_plane(piece, head_ext)
    rel = stats_of(gathered.reshape(-1, gathered.shape[-1])).reshape(4, 4, 4, rows)
    arrived = exchange_plane(jnp.moveaxis(rel, 0, 2))
    own = jnp.stack(merge(arrived.reshape(16, 4, rows), axis=0))
    everyone = exchange_tp(own, n_tp)
    top, weight_sum, weighted, picked = merge(everyone, axis=0)
    log_norm = top + jnp.log(weight_sum)
    live = jnp.arange(rows, dtype=jnp.int32) < lengths[0]
    logprob = jnp.where(live, picked - log_norm, jnp.float32(0.0))
    entropy = jnp.where(live, log_norm - weighted / weight_sum, jnp.float32(0.0))
    mean_lp = (jnp.sum(logprob) / lengths[0].astype(jnp.float32)).reshape(1)
    top_live = jnp.max(jnp.where(live, top, jnp.float32(-1e30))).reshape(1)
    return (logprob, entropy, mean_lp, top_live)


def solution(mesh):
    n_req, n_tp = mesh.devices.shape
    devices = np.asarray(mesh.devices).reshape(4, n_req // 8, 2, n_tp)
    fine = Mesh(devices, ("x", "z", "core", "tp"))
    rq = ("x", "z", "core")
    in_specs = (P(rq, None), P(), P(None, (*rq, "tp")), P(rq), P(rq))
    out_specs = (P(rq), P(rq), P(rq), P(rq))
    return jax.shard_map(
        per_device, mesh=fine, in_specs=in_specs, out_specs=out_specs, check_vma=False
    )
```

```python
import functools

import jax
import jax.numpy as jnp
import numpy as np
from jax import lax
from jax.experimental import pallas as pl
from jax.experimental.pallas import tpu as pltpu
from jax.sharding import Mesh, PartitionSpec as P

MESH = pl.DeviceIdType.MESH
EXTRA = 128


def slice_stats(block, target, matrix, vocab_ids):
    logits = jnp.dot(block, matrix, preferred_element_type=jnp.float32)
    top = jnp.max(logits, axis=-1)
    shifted = jnp.exp(logits - top[:, None])
    weight_sum = jnp.sum(shifted, axis=-1)
    weighted = jnp.sum(shifted * logits, axis=-1)
    hit = vocab_ids == target[:, None]
    picked = jnp.sum(jnp.where(hit, logits, 0.0), axis=-1)
    return jnp.stack([top, weight_sum, weighted, picked])


def merge(stats, axis):
    top = jnp.max(stats[:, 0], axis=axis)
    factor = jnp.exp(stats[:, 0] - jnp.expand_dims(top, axis))
    return (
        top,
        jnp.sum(stats[:, 1] * factor, axis=axis),
        jnp.sum(stats[:, 2] * factor, axis=axis),
        jnp.sum(stats[:, 3], axis=axis),
    )


def fused_kernel(n_tp, piece_ref, head_ref, sel_ref, out_ref, stats_ref,
                 hboth, vbuf, local_sems, head_sems, send_sems, recv_sems, load_sems):
    xi, zi = lax.axis_index("x"), lax.axis_index("z")
    core, tp = lax.axis_index("core"), lax.axis_index("tp")
    vdev = head_ref.shape[0]

    def dev(dx, dz):
        return (lax.rem(xi + dx, 4), lax.rem(zi + dz, 4), core, tp)

    partner = (xi, zi, 1 - core, tp)
    barrier = pltpu.get_barrier_semaphore()
    for dx, dz in ((1, 0), (3, 0), (0, 1), (0, 3)):
        pl.semaphore_signal(barrier, inc=1, device_id=dev(dx, dz), device_id_type=MESH)
    pl.semaphore_signal(barrier, inc=1, device_id=partner, device_id_type=MESH)
    pl.semaphore_wait(barrier, 5)
    mine = pl.ds(pl.multiple_of(core * vdev, vdev), vdev)
    swap = pltpu.make_async_remote_copy(
        src_ref=head_ref,
        dst_ref=hboth.at[mine],
        send_sem=head_sems.at[0],
        recv_sem=head_sems.at[1],
        device_id=partner,
        device_id_type=MESH,
    )
    swap.start()
    own_head = pltpu.make_async_copy(head_ref, hboth.at[mine], local_sems.at[0])
    own_head.start()
    sel = pltpu.make_async_copy(sel_ref, hboth.at[pl.ds(2 * vdev, sel_ref.shape[0])], local_sems.at[1])
    sel.start()
    own = pltpu.make_async_copy(piece_ref, out_ref.at[0, 0], local_sems.at[2])
    own.start()
    rows = piece_ref.shape[0]
    h, q = rows // 2, rows // 4
    count = [0]

    def send(src, dst, dx, dz):
        k = count[0]
        count[0] += 1
        cp = pltpu.make_async_remote_copy(
            src_ref=src,
            dst_ref=dst,
            send_sem=send_sems.at[k],
            recv_sem=recv_sems.at[k],
            device_id=dev(dx, dz),
            device_id_type=MESH,
        )
        cp.start()
        return cp

    def finish(cps):
        for cp in cps:
            cp.wait()

    chip = xi * 4 + zi
    ids = lax.broadcasted_iota(jnp.int32, (2 * vdev, 1), 0)
    vocab = (((chip * 2 + ids // vdev) * n_tp + tp) * vdev + ids % vdev).astype(jnp.float32)

    def group(m, half):
        off = lax.rem(m * 3, 4)
        loads = []
        for j in range(4):
            if half == 0:
                src = out_ref.at[off, j, pl.ds(0, h)]
            else:
                src = out_ref.at[j, off, pl.ds(h, h)]
            cp = pltpu.make_async_copy(src, vbuf.at[j], load_sems.at[j])
            cp.start()
            loads.append(cp)
        finish(loads)
        block = vbuf[...].reshape(4 * h, vbuf.shape[2])
        logits = lax.dot_general(
            hboth[...], block, (((1,), (1,)), ((), ())), preferred_element_type=jnp.float32
        )
        real = logits[: 2 * vdev]
        code = logits[2 * vdev: 2 * vdev + 8]
        target = code[0:1] + code[1:2] * 64.0 + code[2:3] * 4096.0
        top = jnp.max(real, axis=0, keepdims=True)
        shifted = jnp.exp(real - top)
        g = m * 2 + half
        stats_ref[g, 0:1, :] = top
        stats_ref[g, 1:2, :] = jnp.sum(shifted, axis=0, keepdims=True)
        stats_ref[g, 2:3, :] = jnp.sum(shifted * real, axis=0, keepdims=True)
        stats_ref[g, 3:4, :] = jnp.sum(jnp.where(vocab == target, real, 0.0), axis=0, keepdims=True)

    def phase(ms):
        def body(i, carry):
            m = ms[0] + i * (ms[1] - ms[0]) if len(ms) > 1 else ms[0] + i * 0
            group(m, 0)
            group(m, 1)
            return carry

        lax.fori_loop(0, len(ms), body, 0)

    finish([
        send(piece_ref.at[0:h], out_ref.at[0, 3, 0:h], 1, 0),
        send(piece_ref.at[0:h], out_ref.at[0, 1, 0:h], 3, 0),
        send(piece_ref.at[h:rows], out_ref.at[3, 0, h:rows], 0, 1),
        send(piece_ref.at[h:rows], out_ref.at[1, 0, h:rows], 0, 3),
    ])
    finish([
        send(out_ref.at[0, 3, 0:q], out_ref.at[0, 2, 0:q], 1, 0),
        send(out_ref.at[0, 1, q:h], out_ref.at[0, 2, q:h], 3, 0),
        send(out_ref.at[3, 0, h:h + q], out_ref.at[2, 0, h:h + q], 0, 1),
        send(out_ref.at[1, 0, h + q:rows], out_ref.at[2, 0, h + q:rows], 0, 3),
    ])
    own.wait()
    third = [
        send(out_ref.at[0, :, 0:h], out_ref.at[3, :, 0:h], 0, 1),
        send(out_ref.at[0, :, 0:h], out_ref.at[1, :, 0:h], 0, 3),
        send(out_ref.at[:, 0, h:rows], out_ref.at[:, 3, h:rows], 1, 0),
        send(out_ref.at[:, 0, h:rows], out_ref.at[:, 1, h:rows], 3, 0),
    ]
    swap.wait()
    own_head.wait()
    sel.wait()
    phase((0,))
    finish(third)
    fourth = [
        send(out_ref.at[3, :, 0:q], out_ref.at[2, :, 0:q], 0, 1),
        send(out_ref.at[1, :, q:h], out_ref.at[2, :, q:h], 0, 3),
        send(out_ref.at[:, 3, h:h + q], out_ref.at[:, 2, h:h + q], 1, 0),
        send(out_ref.at[:, 1, h + q:rows], out_ref.at[:, 2, h + q:rows], 3, 0),
    ]
    phase((1, 3))
    finish(fourth)
    phase((2,))


def gather_and_stats(piece, head_t, sel, n_tp):
    rows, cols = piece.shape
    vdev = head_t.shape[0]
    h = rows // 2
    return pl.pallas_call(
        functools.partial(fused_kernel, n_tp),
        out_shape=(
            jax.ShapeDtypeStruct((4, 4, rows, cols), piece.dtype),
            jax.ShapeDtypeStruct((8, 8, 4 * h), jnp.float32),
        ),
        in_specs=[pl.BlockSpec(memory_space=pl.ANY)] * 3,
        out_specs=(pl.BlockSpec(memory_space=pl.ANY), pl.BlockSpec(memory_space=pltpu.VMEM)),
        scratch_shapes=[
            pltpu.VMEM((2 * vdev + sel.shape[0], cols), jnp.bfloat16),
            pltpu.VMEM((4, h, cols), jnp.bfloat16),
            pltpu.SemaphoreType.DMA((3,)),
            pltpu.SemaphoreType.DMA((2,)),
            pltpu.SemaphoreType.DMA((16,)),
            pltpu.SemaphoreType.DMA((16,)),
            pltpu.SemaphoreType.DMA((4,)),
        ],
        compiler_params=pltpu.CompilerParams(
            collective_id=1, has_side_effects=True, vmem_limit_bytes=60 * 1024 * 1024
        ),
    )(piece, head_t, sel)


def plane_kernel(stats_ref, out_ref, own_sem, send_sems, recv_sems):
    xi, zi = lax.axis_index("x"), lax.axis_index("z")
    core, tp = lax.axis_index("core"), lax.axis_index("tp")
    offsets = [(dx, dz) for dz in range(4) for dx in range(4) if dx or dz]
    barrier = pltpu.get_barrier_semaphore()
    for dx, dz in offsets:
        peer = (lax.rem(xi + dx, 4), lax.rem(zi + dz, 4), core, tp)
        pl.semaphore_signal(barrier, inc=1, device_id=peer, device_id_type=MESH)
    pl.semaphore_wait(barrier, len(offsets))
    own = pltpu.make_async_copy(stats_ref.at[0, 0], out_ref.at[0, 0], own_sem)
    own.start()
    cps = []
    for k, (dx, dz) in enumerate(offsets):
        peer = (lax.rem(xi + dx, 4), lax.rem(zi + dz, 4), core, tp)
        cp = pltpu.make_async_remote_copy(
            src_ref=stats_ref.at[dz, dx],
            dst_ref=out_ref.at[(4 - dz) % 4, (4 - dx) % 4],
            send_sem=send_sems.at[k],
            recv_sem=recv_sems.at[k],
            device_id=peer,
            device_id_type=MESH,
        )
        cp.start()
        cps.append(cp)
    own.wait()
    for cp in cps:
        cp.wait()


def exchange_plane(stats):
    return pl.pallas_call(
        plane_kernel,
        out_shape=jax.ShapeDtypeStruct(stats.shape, stats.dtype),
        in_specs=[pl.BlockSpec(memory_space=pl.ANY)],
        out_specs=pl.BlockSpec(memory_space=pl.ANY),
        scratch_shapes=[
            pltpu.SemaphoreType.DMA,
            pltpu.SemaphoreType.DMA((15,)),
            pltpu.SemaphoreType.DMA((15,)),
        ],
        compiler_params=pltpu.CompilerParams(collective_id=2, has_side_effects=True),
    )(stats)


def tp_kernel(own_ref, out_ref, own_sem, send_sems, recv_sems):
    xi, zi = lax.axis_index("x"), lax.axis_index("z")
    core, tp = lax.axis_index("core"), lax.axis_index("tp")
    n = out_ref.shape[0]
    barrier = pltpu.get_barrier_semaphore()
    for d in range(1, n):
        peer = (xi, zi, core, lax.rem(tp + d, n))
        pl.semaphore_signal(barrier, inc=1, device_id=peer, device_id_type=MESH)
    pl.semaphore_wait(barrier, n - 1)
    own = pltpu.make_async_copy(own_ref, out_ref.at[tp], own_sem)
    own.start()
    cps = []
    for d in range(1, n):
        peer = (xi, zi, core, lax.rem(tp + d, n))
        cp = pltpu.make_async_remote_copy(
            src_ref=own_ref,
            dst_ref=out_ref.at[tp],
            send_sem=send_sems.at[d - 1],
            recv_sem=recv_sems.at[d - 1],
            device_id=peer,
            device_id_type=MESH,
        )
        cp.start()
        cps.append(cp)
    own.wait()
    for cp in cps:
        cp.wait()


def exchange_tp(own, n_tp):
    return pl.pallas_call(
        tp_kernel,
        out_shape=jax.ShapeDtypeStruct((n_tp, *own.shape), own.dtype),
        in_specs=[pl.BlockSpec(memory_space=pl.ANY)],
        out_specs=pl.BlockSpec(memory_space=pl.ANY),
        scratch_shapes=[
            pltpu.SemaphoreType.DMA,
            pltpu.SemaphoreType.DMA((n_tp - 1,)),
            pltpu.SemaphoreType.DMA((n_tp - 1,)),
        ],
        compiler_params=pltpu.CompilerParams(collective_id=3, has_side_effects=True),
    )(own)


def per_device(hidden_states, norm_gain, head, target_ids, lengths):
    feats = hidden_states.astype(jnp.float32)
    scale = lax.rsqrt(jnp.mean(feats * feats, axis=-1, keepdims=True) + 1e-06)
    normed = (feats * scale * norm_gain).astype(jnp.bfloat16)
    rows, dim = normed.shape
    vdev = head.shape[1]
    n_tp = lax.axis_size("tp")
    xi = lax.axis_index("x")
    zi = lax.axis_index("z")
    core = lax.axis_index("core")
    tp = lax.axis_index("tp")
    n_z = lax.axis_size("z")
    chip = xi * n_z + zi
    digits = jnp.stack([target_ids % 64, (target_ids // 64) % 64, target_ids // 4096], axis=1)
    tail = jnp.zeros((rows, EXTRA), jnp.bfloat16).at[:, :3].set(digits.astype(jnp.bfloat16))
    piece = jnp.concatenate([normed, tail], axis=1)
    head_t = jnp.concatenate([head, jnp.zeros((EXTRA, vdev), head.dtype)], axis=0).T
    sel = jnp.zeros((8, dim + EXTRA), jnp.bfloat16).at[jnp.arange(3), dim + jnp.arange(3)].set(1.0)
    _, stats = gather_and_stats(piece, head_t, sel, n_tp)
    h = rows // 2
    order = jnp.array([0, 3, 2, 1])
    st = stats[:, :4].reshape(4, 2, 4, 4, h)
    s_a = jnp.transpose(st[:, 0], (1, 0, 2, 3))[:, order]
    s_b = jnp.transpose(st[:, 1], (1, 2, 0, 3))[:, :, order]
    rel = jnp.concatenate([s_a, s_b], axis=3)
    arrived = exchange_plane(jnp.moveaxis(rel, 0, 2))
    own = jnp.stack(merge(arrived.reshape(16, 4, rows), axis=0))
    everyone = exchange_tp(own, n_tp)
    top, weight_sum, weighted, picked = merge(everyone, axis=0)
    log_norm = top + jnp.log(weight_sum)
    live = jnp.arange(rows, dtype=jnp.int32) < lengths[0]
    logprob = jnp.where(live, picked - log_norm, jnp.float32(0.0))
    entropy = jnp.where(live, log_norm - weighted / weight_sum, jnp.float32(0.0))
    mean_lp = (jnp.sum(logprob) / lengths[0].astype(jnp.float32)).reshape(1)
    top_live = jnp.max(jnp.where(live, top, jnp.float32(-1e30))).reshape(1)
    return (logprob, entropy, mean_lp, top_live)


def solution(mesh):
    n_req, n_tp = mesh.devices.shape
    devices = np.asarray(mesh.devices).reshape(4, n_req // 8, 2, n_tp)
    fine = Mesh(devices, ("x", "z", "core", "tp"))
    rq = ("x", "z", "core")
    in_specs = (P(rq, None), P(), P(None, (*rq, "tp")), P(rq), P(rq))
    out_specs = (P(rq), P(rq), P(rq), P(rq))
    return jax.shard_map(
        per_device, mesh=fine, in_specs=in_specs, out_specs=out_specs, check_vma=False
    )
```

```python
import functools

import jax
import jax.numpy as jnp
import numpy as np
from jax import lax
from jax.experimental import pallas as pl
from jax.experimental.pallas import tpu as pltpu
from jax.sharding import Mesh, PartitionSpec as P

MESH = pl.DeviceIdType.MESH
EXTRA = 128


def slice_stats(block, target, matrix, vocab_ids):
    logits = jnp.dot(block, matrix, preferred_element_type=jnp.float32)
    top = jnp.max(logits, axis=-1)
    shifted = jnp.exp(logits - top[:, None])
    weight_sum = jnp.sum(shifted, axis=-1)
    weighted = jnp.sum(shifted * logits, axis=-1)
    hit = vocab_ids == target[:, None]
    picked = jnp.sum(jnp.where(hit, logits, 0.0), axis=-1)
    return jnp.stack([top, weight_sum, weighted, picked])


def merge(stats, axis):
    top = jnp.max(stats[:, 0], axis=axis)
    factor = jnp.exp(stats[:, 0] - jnp.expand_dims(top, axis))
    return (
        top,
        jnp.sum(stats[:, 1] * factor, axis=axis),
        jnp.sum(stats[:, 2] * factor, axis=axis),
        jnp.sum(stats[:, 3], axis=axis),
    )


def fused_kernel(n_tp, piece_ref, head_ref, sel_ref, out_ref, stats_ref,
                 hboth, vbuf, local_sems, head_sems, send_sems, recv_sems, load_sems):
    xi, zi = lax.axis_index("x"), lax.axis_index("z")
    core, tp = lax.axis_index("core"), lax.axis_index("tp")
    vdev = head_ref.shape[0]

    def dev(dx, dz):
        return (lax.rem(xi + dx, 4), lax.rem(zi + dz, 4), core, tp)

    partner = (xi, zi, 1 - core, tp)
    barrier = pltpu.get_barrier_semaphore()
    for dx, dz in ((1, 0), (3, 0), (0, 1), (0, 3)):
        pl.semaphore_signal(barrier, inc=1, device_id=dev(dx, dz), device_id_type=MESH)
    pl.semaphore_signal(barrier, inc=1, device_id=partner, device_id_type=MESH)
    pl.semaphore_wait(barrier, 5)
    mine = pl.ds(pl.multiple_of(core * vdev, vdev), vdev)
    swap = pltpu.make_async_remote_copy(
        src_ref=head_ref,
        dst_ref=hboth.at[mine],
        send_sem=head_sems.at[0],
        recv_sem=head_sems.at[1],
        device_id=partner,
        device_id_type=MESH,
    )
    swap.start()
    own_head = pltpu.make_async_copy(head_ref, hboth.at[mine], local_sems.at[0])
    own_head.start()
    sel = pltpu.make_async_copy(sel_ref, hboth.at[pl.ds(2 * vdev, sel_ref.shape[0])], local_sems.at[1])
    sel.start()
    own = pltpu.make_async_copy(piece_ref, out_ref.at[0, 0], local_sems.at[2])
    own.start()
    rows = piece_ref.shape[0]
    h, q = rows // 2, rows // 4
    count = [0]

    def send(src, dst, dx, dz):
        k = count[0]
        count[0] += 1
        cp = pltpu.make_async_remote_copy(
            src_ref=src,
            dst_ref=dst,
            send_sem=send_sems.at[k],
            recv_sem=recv_sems.at[k],
            device_id=dev(dx, dz),
            device_id_type=MESH,
        )
        cp.start()
        return cp

    def finish(cps):
        for cp in cps:
            cp.wait()

    chip = xi * 4 + zi
    ids = lax.broadcasted_iota(jnp.int32, (2 * vdev, 1), 0)
    vocab = (((chip * 2 + ids // vdev) * n_tp + tp) * vdev + ids % vdev).astype(jnp.float32)

    def group(off, half, sub):
        loads = []
        r0 = half * h + sub * q
        for j in range(4):
            dz = off * (1 - half) + j * half
            dx = j * (1 - half) + off * half
            cp = pltpu.make_async_copy(out_ref.at[dz, dx, pl.ds(r0, q)], vbuf.at[j], load_sems.at[j])
            cp.start()
            loads.append(cp)
        finish(loads)
        block = vbuf[...].reshape(4 * q, vbuf.shape[2])
        logits = lax.dot_general(
            hboth[...], block, (((1,), (1,)), ((), ())), preferred_element_type=jnp.float32
        )
        real = logits[: 2 * vdev]
        code = logits[2 * vdev: 2 * vdev + 8]
        target = code[0:1] + code[1:2] * 64.0 + code[2:3] * 4096.0
        top = jnp.max(real, axis=0, keepdims=True)
        shifted = jnp.exp(real - top)
        g = (off * 2 + half) * 2 + sub
        stats_ref[g, 0:1, :] = top
        stats_ref[g, 1:2, :] = jnp.sum(shifted, axis=0, keepdims=True)
        stats_ref[g, 2:3, :] = jnp.sum(shifted * real, axis=0, keepdims=True)
        stats_ref[g, 3:4, :] = jnp.sum(jnp.where(vocab == target, real, 0.0), axis=0, keepdims=True)

    def run(count, pick):
        def body(i, carry):
            group(*pick(i))
            return carry

        lax.fori_loop(0, count, body, 0)

    finish([
        send(piece_ref.at[0:h], out_ref.at[0, 3, 0:h], 1, 0),
        send(piece_ref.at[0:h], out_ref.at[0, 1, 0:h], 3, 0),
        send(piece_ref.at[h:rows], out_ref.at[3, 0, h:rows], 0, 1),
        send(piece_ref.at[h:rows], out_ref.at[1, 0, h:rows], 0, 3),
    ])
    finish([
        send(out_ref.at[0, 3, 0:q], out_ref.at[0, 2, 0:q], 1, 0),
        send(out_ref.at[0, 1, q:h], out_ref.at[0, 2, q:h], 3, 0),
        send(out_ref.at[3, 0, h:h + q], out_ref.at[2, 0, h:h + q], 0, 1),
        send(out_ref.at[1, 0, h + q:rows], out_ref.at[2, 0, h + q:rows], 0, 3),
    ])
    own.wait()
    third = []
    for lo, hi in ((0, q), (q, h)):
        third.append([
            send(out_ref.at[0, :, lo:hi], out_ref.at[3, :, lo:hi], 0, 1),
            send(out_ref.at[0, :, lo:hi], out_ref.at[1, :, lo:hi], 0, 3),
            send(out_ref.at[:, 0, h + lo:h + hi], out_ref.at[:, 3, h + lo:h + hi], 1, 0),
            send(out_ref.at[:, 0, h + lo:h + hi], out_ref.at[:, 1, h + lo:h + hi], 3, 0),
        ])
    swap.wait()
    own_head.wait()
    sel.wait()
    run(4, lambda i: (0, i // 2, i % 2))
    finish(third[0])
    fourth_a = [
        send(out_ref.at[3, :, 0:q], out_ref.at[2, :, 0:q], 0, 1),
        send(out_ref.at[:, 3, h:h + q], out_ref.at[:, 2, h:h + q], 1, 0),
    ]
    run(4, lambda i: (3 - 2 * (i % 2), i // 2, 0))
    finish(third[1])
    fourth_b = [
        send(out_ref.at[1, :, q:h], out_ref.at[2, :, q:h], 0, 3),
        send(out_ref.at[:, 1, h + q:rows], out_ref.at[:, 2, h + q:rows], 3, 0),
    ]
    run(4, lambda i: (3 - 2 * (i % 2), i // 2, 1))
    finish(fourth_a)
    run(2, lambda i: (2, i, 0))
    finish(fourth_b)
    run(2, lambda i: (2, i, 1))


def gather_and_stats(piece, head_t, sel, n_tp):
    rows, cols = piece.shape
    vdev = head_t.shape[0]
    h = rows // 2
    return pl.pallas_call(
        functools.partial(fused_kernel, n_tp),
        out_shape=(
            jax.ShapeDtypeStruct((4, 4, rows, cols), piece.dtype),
            jax.ShapeDtypeStruct((16, 8, 2 * h), jnp.float32),
        ),
        in_specs=[pl.BlockSpec(memory_space=pl.ANY)] * 3,
        out_specs=(pl.BlockSpec(memory_space=pl.ANY), pl.BlockSpec(memory_space=pltpu.VMEM)),
        scratch_shapes=[
            pltpu.VMEM((2 * vdev + sel.shape[0], cols), jnp.bfloat16),
            pltpu.VMEM((4, h // 2, cols), jnp.bfloat16),
            pltpu.SemaphoreType.DMA((3,)),
            pltpu.SemaphoreType.DMA((2,)),
            pltpu.SemaphoreType.DMA((20,)),
            pltpu.SemaphoreType.DMA((20,)),
            pltpu.SemaphoreType.DMA((4,)),
        ],
        compiler_params=pltpu.CompilerParams(
            collective_id=1, has_side_effects=True, vmem_limit_bytes=60 * 1024 * 1024
        ),
    )(piece, head_t, sel)


def plane_kernel(stats_ref, out_ref, own_sem, send_sems, recv_sems):
    xi, zi = lax.axis_index("x"), lax.axis_index("z")
    core, tp = lax.axis_index("core"), lax.axis_index("tp")
    offsets = [(dx, dz) for dz in range(4) for dx in range(4) if dx or dz]
    barrier = pltpu.get_barrier_semaphore()
    for dx, dz in offsets:
        peer = (lax.rem(xi + dx, 4), lax.rem(zi + dz, 4), core, tp)
        pl.semaphore_signal(barrier, inc=1, device_id=peer, device_id_type=MESH)
    pl.semaphore_wait(barrier, len(offsets))
    own = pltpu.make_async_copy(stats_ref.at[0, 0], out_ref.at[0, 0], own_sem)
    own.start()
    cps = []
    for k, (dx, dz) in enumerate(offsets):
        peer = (lax.rem(xi + dx, 4), lax.rem(zi + dz, 4), core, tp)
        cp = pltpu.make_async_remote_copy(
            src_ref=stats_ref.at[dz, dx],
            dst_ref=out_ref.at[(4 - dz) % 4, (4 - dx) % 4],
            send_sem=send_sems.at[k],
            recv_sem=recv_sems.at[k],
            device_id=peer,
            device_id_type=MESH,
        )
        cp.start()
        cps.append(cp)
    own.wait()
    for cp in cps:
        cp.wait()


def exchange_plane(stats):
    return pl.pallas_call(
        plane_kernel,
        out_shape=jax.ShapeDtypeStruct(stats.shape, stats.dtype),
        in_specs=[pl.BlockSpec(memory_space=pl.ANY)],
        out_specs=pl.BlockSpec(memory_space=pl.ANY),
        scratch_shapes=[
            pltpu.SemaphoreType.DMA,
            pltpu.SemaphoreType.DMA((15,)),
            pltpu.SemaphoreType.DMA((15,)),
        ],
        compiler_params=pltpu.CompilerParams(collective_id=2, has_side_effects=True),
    )(stats)


def tp_kernel(own_ref, out_ref, own_sem, send_sems, recv_sems):
    xi, zi = lax.axis_index("x"), lax.axis_index("z")
    core, tp = lax.axis_index("core"), lax.axis_index("tp")
    n = out_ref.shape[0]
    barrier = pltpu.get_barrier_semaphore()
    for d in range(1, n):
        peer = (xi, zi, core, lax.rem(tp + d, n))
        pl.semaphore_signal(barrier, inc=1, device_id=peer, device_id_type=MESH)
    pl.semaphore_wait(barrier, n - 1)
    own = pltpu.make_async_copy(own_ref, out_ref.at[tp], own_sem)
    own.start()
    cps = []
    for d in range(1, n):
        peer = (xi, zi, core, lax.rem(tp + d, n))
        cp = pltpu.make_async_remote_copy(
            src_ref=own_ref,
            dst_ref=out_ref.at[tp],
            send_sem=send_sems.at[d - 1],
            recv_sem=recv_sems.at[d - 1],
            device_id=peer,
            device_id_type=MESH,
        )
        cp.start()
        cps.append(cp)
    own.wait()
    for cp in cps:
        cp.wait()


def exchange_tp(own, n_tp):
    return pl.pallas_call(
        tp_kernel,
        out_shape=jax.ShapeDtypeStruct((n_tp, *own.shape), own.dtype),
        in_specs=[pl.BlockSpec(memory_space=pl.ANY)],
        out_specs=pl.BlockSpec(memory_space=pl.ANY),
        scratch_shapes=[
            pltpu.SemaphoreType.DMA,
            pltpu.SemaphoreType.DMA((n_tp - 1,)),
            pltpu.SemaphoreType.DMA((n_tp - 1,)),
        ],
        compiler_params=pltpu.CompilerParams(collective_id=3, has_side_effects=True),
    )(own)


def per_device(hidden_states, norm_gain, head, target_ids, lengths):
    feats = hidden_states.astype(jnp.float32)
    scale = lax.rsqrt(jnp.mean(feats * feats, axis=-1, keepdims=True) + 1e-06)
    normed = (feats * scale * norm_gain).astype(jnp.bfloat16)
    rows, dim = normed.shape
    vdev = head.shape[1]
    n_tp = lax.axis_size("tp")
    xi = lax.axis_index("x")
    zi = lax.axis_index("z")
    core = lax.axis_index("core")
    tp = lax.axis_index("tp")
    n_z = lax.axis_size("z")
    chip = xi * n_z + zi
    digits = jnp.stack([target_ids % 64, (target_ids // 64) % 64, target_ids // 4096], axis=1)
    tail = jnp.zeros((rows, EXTRA), jnp.bfloat16).at[:, :3].set(digits.astype(jnp.bfloat16))
    piece = jnp.concatenate([normed, tail], axis=1)
    head_t = jnp.concatenate([head, jnp.zeros((EXTRA, vdev), head.dtype)], axis=0).T
    sel = jnp.zeros((8, dim + EXTRA), jnp.bfloat16).at[jnp.arange(3), dim + jnp.arange(3)].set(1.0)
    _, stats = gather_and_stats(piece, head_t, sel, n_tp)
    q = rows // 4
    st = stats[:, :4].reshape(4, 2, 2, 4, 4, q)
    s_a = jnp.transpose(st[:, 0], (2, 0, 3, 1, 4)).reshape(4, 4, 4, 2 * q)
    s_b = jnp.transpose(st[:, 1], (2, 3, 0, 1, 4)).reshape(4, 4, 4, 2 * q)
    rel = jnp.concatenate([s_a, s_b], axis=3)
    arrived = exchange_plane(jnp.moveaxis(rel, 0, 2))
    own = jnp.stack(merge(arrived.reshape(16, 4, rows), axis=0))
    everyone = exchange_tp(own, n_tp)
    top, weight_sum, weighted, picked = merge(everyone, axis=0)
    log_norm = top + jnp.log(weight_sum)
    live = jnp.arange(rows, dtype=jnp.int32) < lengths[0]
    logprob = jnp.where(live, picked - log_norm, jnp.float32(0.0))
    entropy = jnp.where(live, log_norm - weighted / weight_sum, jnp.float32(0.0))
    mean_lp = (jnp.sum(logprob) / lengths[0].astype(jnp.float32)).reshape(1)
    top_live = jnp.max(jnp.where(live, top, jnp.float32(-1e30))).reshape(1)
    return (logprob, entropy, mean_lp, top_live)


def solution(mesh):
    n_req, n_tp = mesh.devices.shape
    devices = np.asarray(mesh.devices).reshape(4, n_req // 8, 2, n_tp)
    fine = Mesh(devices, ("x", "z", "core", "tp"))
    rq = ("x", "z", "core")
    in_specs = (P(rq, None), P(), P(None, (*rq, "tp")), P(rq), P(rq))
    out_specs = (P(rq), P(rq), P(rq), P(rq))
    return jax.shard_map(
        per_device, mesh=fine, in_specs=in_specs, out_specs=out_specs, check_vma=False
    )
```

```python
import functools

import jax
import jax.numpy as jnp
import numpy as np
from jax import lax
from jax.experimental import pallas as pl
from jax.experimental.pallas import tpu as pltpu
from jax.sharding import Mesh, PartitionSpec as P

MESH = pl.DeviceIdType.MESH
EXTRA = 128


def slice_stats(block, target, matrix, vocab_ids):
    logits = jnp.dot(block, matrix, preferred_element_type=jnp.float32)
    top = jnp.max(logits, axis=-1)
    shifted = jnp.exp(logits - top[:, None])
    weight_sum = jnp.sum(shifted, axis=-1)
    weighted = jnp.sum(shifted * logits, axis=-1)
    hit = vocab_ids == target[:, None]
    picked = jnp.sum(jnp.where(hit, logits, 0.0), axis=-1)
    return jnp.stack([top, weight_sum, weighted, picked])


def merge(stats, axis):
    top = jnp.max(stats[:, 0], axis=axis)
    factor = jnp.exp(stats[:, 0] - jnp.expand_dims(top, axis))
    return (
        top,
        jnp.sum(stats[:, 1] * factor, axis=axis),
        jnp.sum(stats[:, 2] * factor, axis=axis),
        jnp.sum(stats[:, 3], axis=axis),
    )


def fused_kernel(n_tp, piece_ref, head_ref, tin_ref, out_ref, stats_ref,
                 hboth, vbuf, tgt, local_sems, head_sems, send_sems, recv_sems, load_sems):
    xi, zi = lax.axis_index("x"), lax.axis_index("z")
    core, tp = lax.axis_index("core"), lax.axis_index("tp")
    vdev = head_ref.shape[0]

    def dev(dx, dz):
        return (lax.rem(xi + dx, 4), lax.rem(zi + dz, 4), core, tp)

    partner = (xi, zi, 1 - core, tp)
    barrier = pltpu.get_barrier_semaphore()
    for dx, dz in ((1, 0), (3, 0), (0, 1), (0, 3)):
        pl.semaphore_signal(barrier, inc=1, device_id=dev(dx, dz), device_id_type=MESH)
    pl.semaphore_signal(barrier, inc=1, device_id=partner, device_id_type=MESH)
    pl.semaphore_wait(barrier, 5)
    mine = pl.ds(pl.multiple_of(core * vdev, vdev), vdev)
    swap = pltpu.make_async_remote_copy(
        src_ref=head_ref,
        dst_ref=hboth.at[mine],
        send_sem=head_sems.at[0],
        recv_sem=head_sems.at[1],
        device_id=partner,
        device_id_type=MESH,
    )
    swap.start()
    own_head = pltpu.make_async_copy(head_ref, hboth.at[mine], local_sems.at[0])
    own_head.start()
    sel = pltpu.make_async_copy(tin_ref, tgt.at[0, 0], local_sems.at[1])
    sel.start()
    own = pltpu.make_async_copy(piece_ref, out_ref.at[0, 0], local_sems.at[2])
    own.start()
    rows = piece_ref.shape[0]
    h, q = rows // 2, rows // 4
    count = [0]

    def send(src, dst, dx, dz):
        k = count[0]
        count[0] += 1
        cp = pltpu.make_async_remote_copy(
            src_ref=src,
            dst_ref=dst,
            send_sem=send_sems.at[k],
            recv_sem=recv_sems.at[k],
            device_id=dev(dx, dz),
            device_id_type=MESH,
        )
        cp.start()
        return cp

    def finish(cps):
        for cp in cps:
            cp.wait()

    chip = xi * 4 + zi
    ids = lax.broadcasted_iota(jnp.int32, (2 * vdev, 1), 0)
    vocab = (((chip * 2 + ids // vdev) * n_tp + tp) * vdev + ids % vdev).astype(jnp.float32)

    def group(m, half):
        off = lax.rem(m * 3, 4)
        loads = []
        for j in range(4):
            if half == 0:
                src = out_ref.at[off, j, pl.ds(0, h)]
            else:
                src = out_ref.at[j, off, pl.ds(h, h)]
            cp = pltpu.make_async_copy(src, vbuf.at[j], load_sems.at[j])
            cp.start()
            loads.append(cp)
        finish(loads)
        block = vbuf[...].reshape(4 * h, vbuf.shape[2])
        real = lax.dot_general(
            hboth[...], block, (((1,), (1,)), ((), ())), preferred_element_type=jnp.float32
        )
        if half == 0:
            pieces = [tgt[off, j, 0, 0:1, :] for j in range(4)]
        else:
            pieces = [tgt[j, off, 1, 0:1, :] for j in range(4)]
        target = jnp.concatenate(pieces, axis=1)
        top = jnp.max(real, axis=0, keepdims=True)
        shifted = jnp.exp(real - top)
        g = m * 2 + half
        stats_ref[g, 0:1, :] = top
        stats_ref[g, 1:2, :] = jnp.sum(shifted, axis=0, keepdims=True)
        stats_ref[g, 2:3, :] = jnp.sum(shifted * real, axis=0, keepdims=True)
        stats_ref[g, 3:4, :] = jnp.sum(jnp.where(vocab == target, real, 0.0), axis=0, keepdims=True)

    def phase(ms):
        def body(i, carry):
            m = ms[0] + i * (ms[1] - ms[0]) if len(ms) > 1 else ms[0] + i * 0
            group(m, 0)
            group(m, 1)
            return carry

        lax.fori_loop(0, len(ms), body, 0)

    finish([
        send(piece_ref.at[0:h], out_ref.at[0, 3, 0:h], 1, 0),
        send(piece_ref.at[0:h], out_ref.at[0, 1, 0:h], 3, 0),
        send(piece_ref.at[h:rows], out_ref.at[3, 0, h:rows], 0, 1),
        send(piece_ref.at[h:rows], out_ref.at[1, 0, h:rows], 0, 3),
        send(tin_ref.at[0], tgt.at[0, 3, 0], 1, 0),
        send(tin_ref.at[0], tgt.at[0, 1, 0], 3, 0),
        send(tin_ref.at[1], tgt.at[3, 0, 1], 0, 1),
        send(tin_ref.at[1], tgt.at[1, 0, 1], 0, 3),
    ])
    finish([
        send(out_ref.at[0, 3, 0:q], out_ref.at[0, 2, 0:q], 1, 0),
        send(out_ref.at[0, 1, q:h], out_ref.at[0, 2, q:h], 3, 0),
        send(out_ref.at[3, 0, h:h + q], out_ref.at[2, 0, h:h + q], 0, 1),
        send(out_ref.at[1, 0, h + q:rows], out_ref.at[2, 0, h + q:rows], 0, 3),
        send(tgt.at[0, 3, 0], tgt.at[0, 2, 0], 1, 0),
        send(tgt.at[3, 0, 1], tgt.at[2, 0, 1], 0, 1),
    ])
    own.wait()
    sel.wait()
    third = [
        send(out_ref.at[0, :, 0:h], out_ref.at[3, :, 0:h], 0, 1),
        send(out_ref.at[0, :, 0:h], out_ref.at[1, :, 0:h], 0, 3),
        send(out_ref.at[:, 0, h:rows], out_ref.at[:, 3, h:rows], 1, 0),
        send(out_ref.at[:, 0, h:rows], out_ref.at[:, 1, h:rows], 3, 0),
        send(tgt.at[0, :, 0], tgt.at[3, :, 0], 0, 1),
        send(tgt.at[0, :, 0], tgt.at[1, :, 0], 0, 3),
        send(tgt.at[:, 0, 1], tgt.at[:, 3, 1], 1, 0),
        send(tgt.at[:, 0, 1], tgt.at[:, 1, 1], 3, 0),
    ]
    swap.wait()
    own_head.wait()
    phase((0,))
    finish(third)
    fourth = [
        send(out_ref.at[3, :, 0:q], out_ref.at[2, :, 0:q], 0, 1),
        send(out_ref.at[1, :, q:h], out_ref.at[2, :, q:h], 0, 3),
        send(out_ref.at[:, 3, h:h + q], out_ref.at[:, 2, h:h + q], 1, 0),
        send(out_ref.at[:, 1, h + q:rows], out_ref.at[:, 2, h + q:rows], 3, 0),
        send(tgt.at[3, :, 0], tgt.at[2, :, 0], 0, 1),
        send(tgt.at[:, 3, 1], tgt.at[:, 2, 1], 1, 0),
    ]
    phase((1, 3))
    finish(fourth)
    phase((2,))


def gather_and_stats(piece, head_t, tin, n_tp):
    rows, cols = piece.shape
    vdev = head_t.shape[0]
    h = rows // 2
    return pl.pallas_call(
        functools.partial(fused_kernel, n_tp),
        out_shape=(
            jax.ShapeDtypeStruct((4, 4, rows, cols), piece.dtype),
            jax.ShapeDtypeStruct((8, 8, 4 * h), jnp.float32),
        ),
        in_specs=[pl.BlockSpec(memory_space=pl.ANY)] * 3,
        out_specs=(pl.BlockSpec(memory_space=pl.ANY), pl.BlockSpec(memory_space=pltpu.VMEM)),
        scratch_shapes=[
            pltpu.VMEM((2 * vdev, cols), jnp.bfloat16),
            pltpu.VMEM((4, h, cols), jnp.bfloat16),
            pltpu.VMEM((4, 4, 2, 8, h), jnp.float32),
            pltpu.SemaphoreType.DMA((3,)),
            pltpu.SemaphoreType.DMA((2,)),
            pltpu.SemaphoreType.DMA((28,)),
            pltpu.SemaphoreType.DMA((28,)),
            pltpu.SemaphoreType.DMA((4,)),
        ],
        compiler_params=pltpu.CompilerParams(
            collective_id=1, has_side_effects=True, vmem_limit_bytes=60 * 1024 * 1024
        ),
    )(piece, head_t, tin)


def plane_kernel(stats_ref, out_ref, own_sem, send_sems, recv_sems):
    xi, zi = lax.axis_index("x"), lax.axis_index("z")
    core, tp = lax.axis_index("core"), lax.axis_index("tp")
    offsets = [(dx, dz) for dz in range(4) for dx in range(4) if dx or dz]
    barrier = pltpu.get_barrier_semaphore()
    for dx, dz in offsets:
        peer = (lax.rem(xi + dx, 4), lax.rem(zi + dz, 4), core, tp)
        pl.semaphore_signal(barrier, inc=1, device_id=peer, device_id_type=MESH)
    pl.semaphore_wait(barrier, len(offsets))
    own = pltpu.make_async_copy(stats_ref.at[0, 0], out_ref.at[0, 0], own_sem)
    own.start()
    cps = []
    for k, (dx, dz) in enumerate(offsets):
        peer = (lax.rem(xi + dx, 4), lax.rem(zi + dz, 4), core, tp)
        cp = pltpu.make_async_remote_copy(
            src_ref=stats_ref.at[dz, dx],
            dst_ref=out_ref.at[(4 - dz) % 4, (4 - dx) % 4],
            send_sem=send_sems.at[k],
            recv_sem=recv_sems.at[k],
            device_id=peer,
            device_id_type=MESH,
        )
        cp.start()
        cps.append(cp)
    own.wait()
    for cp in cps:
        cp.wait()


def exchange_plane(stats):
    return pl.pallas_call(
        plane_kernel,
        out_shape=jax.ShapeDtypeStruct(stats.shape, stats.dtype),
        in_specs=[pl.BlockSpec(memory_space=pl.ANY)],
        out_specs=pl.BlockSpec(memory_space=pl.ANY),
        scratch_shapes=[
            pltpu.SemaphoreType.DMA,
            pltpu.SemaphoreType.DMA((15,)),
            pltpu.SemaphoreType.DMA((15,)),
        ],
        compiler_params=pltpu.CompilerParams(collective_id=2, has_side_effects=True),
    )(stats)


def tp_kernel(own_ref, out_ref, own_sem, send_sems, recv_sems):
    xi, zi = lax.axis_index("x"), lax.axis_index("z")
    core, tp = lax.axis_index("core"), lax.axis_index("tp")
    n = out_ref.shape[0]
    barrier = pltpu.get_barrier_semaphore()
    for d in range(1, n):
        peer = (xi, zi, core, lax.rem(tp + d, n))
        pl.semaphore_signal(barrier, inc=1, device_id=peer, device_id_type=MESH)
    pl.semaphore_wait(barrier, n - 1)
    own = pltpu.make_async_copy(own_ref, out_ref.at[tp], own_sem)
    own.start()
    cps = []
    for d in range(1, n):
        peer = (xi, zi, core, lax.rem(tp + d, n))
        cp = pltpu.make_async_remote_copy(
            src_ref=own_ref,
            dst_ref=out_ref.at[tp],
            send_sem=send_sems.at[d - 1],
            recv_sem=recv_sems.at[d - 1],
            device_id=peer,
            device_id_type=MESH,
        )
        cp.start()
        cps.append(cp)
    own.wait()
    for cp in cps:
        cp.wait()


def exchange_tp(own, n_tp):
    return pl.pallas_call(
        tp_kernel,
        out_shape=jax.ShapeDtypeStruct((n_tp, *own.shape), own.dtype),
        in_specs=[pl.BlockSpec(memory_space=pl.ANY)],
        out_specs=pl.BlockSpec(memory_space=pl.ANY),
        scratch_shapes=[
            pltpu.SemaphoreType.DMA,
            pltpu.SemaphoreType.DMA((n_tp - 1,)),
            pltpu.SemaphoreType.DMA((n_tp - 1,)),
        ],
        compiler_params=pltpu.CompilerParams(collective_id=3, has_side_effects=True),
    )(own)


def per_device(hidden_states, norm_gain, head, target_ids, lengths):
    feats = hidden_states.astype(jnp.float32)
    scale = lax.rsqrt(jnp.mean(feats * feats, axis=-1, keepdims=True) + 1e-06)
    normed = (feats * scale * norm_gain).astype(jnp.bfloat16)
    rows, dim = normed.shape
    vdev = head.shape[1]
    n_tp = lax.axis_size("tp")
    xi = lax.axis_index("x")
    zi = lax.axis_index("z")
    core = lax.axis_index("core")
    tp = lax.axis_index("tp")
    n_z = lax.axis_size("z")
    chip = xi * n_z + zi
    piece = normed
    head_t = head.T
    tin = jnp.broadcast_to(target_ids.astype(jnp.float32).reshape(2, 1, rows // 2), (2, 8, rows // 2))
    _, stats = gather_and_stats(piece, head_t, tin, n_tp)
    h = rows // 2
    order = jnp.array([0, 3, 2, 1])
    st = stats[:, :4].reshape(4, 2, 4, 4, h)
    s_a = jnp.transpose(st[:, 0], (1, 0, 2, 3))[:, order]
    s_b = jnp.transpose(st[:, 1], (1, 2, 0, 3))[:, :, order]
    rel = jnp.concatenate([s_a, s_b], axis=3)
    arrived = exchange_plane(jnp.moveaxis(rel, 0, 2))
    own = jnp.stack(merge(arrived.reshape(16, 4, rows), axis=0))
    everyone = exchange_tp(own, n_tp)
    top, weight_sum, weighted, picked = merge(everyone, axis=0)
    log_norm = top + jnp.log(weight_sum)
    live = jnp.arange(rows, dtype=jnp.int32) < lengths[0]
    logprob = jnp.where(live, picked - log_norm, jnp.float32(0.0))
    entropy = jnp.where(live, log_norm - weighted / weight_sum, jnp.float32(0.0))
    mean_lp = (jnp.sum(logprob) / lengths[0].astype(jnp.float32)).reshape(1)
    top_live = jnp.max(jnp.where(live, top, jnp.float32(-1e30))).reshape(1)
    return (logprob, entropy, mean_lp, top_live)


def solution(mesh):
    n_req, n_tp = mesh.devices.shape
    devices = np.asarray(mesh.devices).reshape(4, n_req // 8, 2, n_tp)
    fine = Mesh(devices, ("x", "z", "core", "tp"))
    rq = ("x", "z", "core")
    in_specs = (P(rq, None), P(), P(None, (*rq, "tp")), P(rq), P(rq))
    out_specs = (P(rq), P(rq), P(rq), P(rq))
    return jax.shard_map(
        per_device, mesh=fine, in_specs=in_specs, out_specs=out_specs, check_vma=False
    )
```

```python
import functools

import jax
import jax.numpy as jnp
import numpy as np
from jax import lax
from jax.experimental import pallas as pl
from jax.experimental.pallas import tpu as pltpu
from jax.sharding import Mesh, PartitionSpec as P

MESH = pl.DeviceIdType.MESH
EXTRA = 128


def slice_stats(block, target, matrix, vocab_ids):
    logits = jnp.dot(block, matrix, preferred_element_type=jnp.float32)
    top = jnp.max(logits, axis=-1)
    shifted = jnp.exp(logits - top[:, None])
    weight_sum = jnp.sum(shifted, axis=-1)
    weighted = jnp.sum(shifted * logits, axis=-1)
    hit = vocab_ids == target[:, None]
    picked = jnp.sum(jnp.where(hit, logits, 0.0), axis=-1)
    return jnp.stack([top, weight_sum, weighted, picked])


def merge(stats, axis):
    top = jnp.max(stats[:, 0], axis=axis)
    factor = jnp.exp(stats[:, 0] - jnp.expand_dims(top, axis))
    return (
        top,
        jnp.sum(stats[:, 1] * factor, axis=axis),
        jnp.sum(stats[:, 2] * factor, axis=axis),
        jnp.sum(stats[:, 3], axis=axis),
    )


def fused_kernel(n_tp, piece_ref, head_ref, tin_ref, out_ref, stats_ref,
                 hboth, vbuf, tgt, local_sems, head_sems, send_sems, recv_sems, load_sems):
    xi, zi = lax.axis_index("x"), lax.axis_index("z")
    core, tp = lax.axis_index("core"), lax.axis_index("tp")
    vdev = head_ref.shape[0]

    def dev(dx, dz):
        return (lax.rem(xi + dx, 4), lax.rem(zi + dz, 4), core, tp)

    partner = (xi, zi, 1 - core, tp)
    barrier = pltpu.get_barrier_semaphore()
    for dx, dz in ((1, 0), (3, 0), (0, 1), (0, 3)):
        pl.semaphore_signal(barrier, inc=1, device_id=dev(dx, dz), device_id_type=MESH)
    pl.semaphore_signal(barrier, inc=1, device_id=partner, device_id_type=MESH)
    pl.semaphore_wait(barrier, 5)
    mine = pl.ds(pl.multiple_of(core * vdev, vdev), vdev)
    swap = pltpu.make_async_remote_copy(
        src_ref=head_ref,
        dst_ref=hboth.at[mine],
        send_sem=head_sems.at[0],
        recv_sem=head_sems.at[1],
        device_id=partner,
        device_id_type=MESH,
    )
    swap.start()
    own_head = pltpu.make_async_copy(head_ref, hboth.at[mine], local_sems.at[0])
    own_head.start()
    sel = pltpu.make_async_copy(tin_ref, tgt.at[0, 0], local_sems.at[1])
    sel.start()
    own = pltpu.make_async_copy(piece_ref, out_ref.at[0, 0], local_sems.at[2])
    own.start()
    rows = piece_ref.shape[0]
    h, q = rows // 2, rows // 4
    count = [0]

    def send(src, dst, dx, dz):
        k = count[0]
        count[0] += 1
        cp = pltpu.make_async_remote_copy(
            src_ref=src,
            dst_ref=dst,
            send_sem=send_sems.at[k],
            recv_sem=recv_sems.at[k],
            device_id=dev(dx, dz),
            device_id_type=MESH,
        )
        cp.start()
        return cp

    def finish(cps):
        for cp in cps:
            cp.wait()

    chip = xi * 4 + zi
    ids = lax.broadcasted_iota(jnp.int32, (2 * vdev, 1), 0)
    vocab = (((chip * 2 + ids // vdev) * n_tp + tp) * vdev + ids % vdev).astype(jnp.float32)

    def group(m, half):
        off = lax.rem(m * 3, 4)
        loads = []
        for j in range(4):
            if half == 0:
                src = out_ref.at[off, j, pl.ds(0, h)]
            else:
                src = out_ref.at[j, off, pl.ds(h, h)]
            cp = pltpu.make_async_copy(src, vbuf.at[j], load_sems.at[j])
            cp.start()
            loads.append(cp)
        finish(loads)
        block = vbuf[...].reshape(4 * h, vbuf.shape[2])
        real = lax.dot_general(
            hboth[...], block, (((1,), (1,)), ((), ())), preferred_element_type=jnp.float32
        )
        if half == 0:
            pieces = [tgt[off, j, 0, 0:1, :] for j in range(4)]
        else:
            pieces = [tgt[j, off, 1, 0:1, :] for j in range(4)]
        target = jnp.concatenate(pieces, axis=1)
        top = jnp.max(real, axis=0, keepdims=True)
        shifted = jnp.exp(real - top)
        g = m * 2 + half
        stats_ref[g, 0:1, :] = top
        stats_ref[g, 1:2, :] = jnp.sum(shifted, axis=0, keepdims=True)
        stats_ref[g, 2:3, :] = jnp.sum(shifted * real, axis=0, keepdims=True)
        stats_ref[g, 3:4, :] = jnp.sum(jnp.where(vocab == target, real, 0.0), axis=0, keepdims=True)

    def phase(ms):
        def body(i, carry):
            m = ms[0] + i * (ms[1] - ms[0]) if len(ms) > 1 else ms[0] + i * 0
            group(m, 0)
            group(m, 1)
            return carry

        lax.fori_loop(0, len(ms), body, 0)

    finish([
        send(piece_ref.at[0:h], out_ref.at[0, 3, 0:h], 1, 0),
        send(piece_ref.at[0:h], out_ref.at[0, 1, 0:h], 3, 0),
        send(piece_ref.at[h:rows], out_ref.at[3, 0, h:rows], 0, 1),
        send(piece_ref.at[h:rows], out_ref.at[1, 0, h:rows], 0, 3),
        send(tin_ref.at[0], tgt.at[0, 3, 0], 1, 0),
        send(tin_ref.at[0], tgt.at[0, 1, 0], 3, 0),
        send(tin_ref.at[1], tgt.at[3, 0, 1], 0, 1),
        send(tin_ref.at[1], tgt.at[1, 0, 1], 0, 3),
    ])
    finish([
        send(out_ref.at[0, 3, 0:q], out_ref.at[0, 2, 0:q], 1, 0),
        send(out_ref.at[0, 1, q:h], out_ref.at[0, 2, q:h], 3, 0),
        send(out_ref.at[3, 0, h:h + q], out_ref.at[2, 0, h:h + q], 0, 1),
        send(out_ref.at[1, 0, h + q:rows], out_ref.at[2, 0, h + q:rows], 0, 3),
        send(tgt.at[0, 3, 0], tgt.at[0, 2, 0], 1, 0),
        send(tgt.at[3, 0, 1], tgt.at[2, 0, 1], 0, 1),
    ])
    own.wait()
    sel.wait()
    third = [
        send(out_ref.at[0, :, 0:h], out_ref.at[3, :, 0:h], 0, 1),
        send(out_ref.at[0, :, 0:h], out_ref.at[1, :, 0:h], 0, 3),
        send(out_ref.at[:, 0, h:rows], out_ref.at[:, 3, h:rows], 1, 0),
        send(out_ref.at[:, 0, h:rows], out_ref.at[:, 1, h:rows], 3, 0),
        send(tgt.at[0, :, 0], tgt.at[3, :, 0], 0, 1),
        send(tgt.at[0, :, 0], tgt.at[1, :, 0], 0, 3),
        send(tgt.at[:, 0, 1], tgt.at[:, 3, 1], 1, 0),
        send(tgt.at[:, 0, 1], tgt.at[:, 1, 1], 3, 0),
    ]
    swap.wait()
    own_head.wait()
    phase((0,))
    finish(third)
    fourth = [
        send(out_ref.at[3, :, 0:q], out_ref.at[2, :, 0:q], 0, 1),
        send(out_ref.at[1, :, q:h], out_ref.at[2, :, q:h], 0, 3),
        send(out_ref.at[:, 3, h:h + q], out_ref.at[:, 2, h:h + q], 1, 0),
        send(out_ref.at[:, 1, h + q:rows], out_ref.at[:, 2, h + q:rows], 3, 0),
        send(tgt.at[3, :, 0], tgt.at[2, :, 0], 0, 1),
        send(tgt.at[:, 3, 1], tgt.at[:, 2, 1], 1, 0),
    ]
    phase((1, 3))
    finish(fourth)
    phase((2,))


def gather_and_stats(piece, head_t, tin, n_tp):
    rows, cols = piece.shape
    vdev = head_t.shape[0]
    h = rows // 2
    return pl.pallas_call(
        functools.partial(fused_kernel, n_tp),
        out_shape=(
            jax.ShapeDtypeStruct((4, 4, rows, cols), piece.dtype),
            jax.ShapeDtypeStruct((8, 8, 4 * h), jnp.float32),
        ),
        in_specs=[pl.BlockSpec(memory_space=pl.ANY)] * 3,
        out_specs=(pl.BlockSpec(memory_space=pl.ANY), pl.BlockSpec(memory_space=pltpu.VMEM)),
        scratch_shapes=[
            pltpu.VMEM((2 * vdev, cols), jnp.bfloat16),
            pltpu.VMEM((4, h, cols), jnp.bfloat16),
            pltpu.VMEM((4, 4, 2, 8, h), jnp.float32),
            pltpu.SemaphoreType.DMA((3,)),
            pltpu.SemaphoreType.DMA((2,)),
            pltpu.SemaphoreType.DMA((28,)),
            pltpu.SemaphoreType.DMA((28,)),
            pltpu.SemaphoreType.DMA((4,)),
        ],
        compiler_params=pltpu.CompilerParams(
            collective_id=1, has_side_effects=True, vmem_limit_bytes=60 * 1024 * 1024
        ),
    )(piece, head_t, tin)


def plane_kernel(n_tp, stats_ref, out_ref, own_sem, send_sems, recv_sems):
    xi, zi = lax.axis_index("x"), lax.axis_index("z")
    core, tp = lax.axis_index("core"), lax.axis_index("tp")
    offsets = [(dx, dz, dy) for dy in range(n_tp) for dz in range(4) for dx in range(4) if dx or dz or dy]

    def peer(dx, dz, dy):
        return (lax.rem(xi + dx, 4), lax.rem(zi + dz, 4), core, lax.rem(tp + dy, n_tp))

    barrier = pltpu.get_barrier_semaphore()
    for dx, dz, dy in offsets:
        pl.semaphore_signal(barrier, inc=1, device_id=peer(dx, dz, dy), device_id_type=MESH)
    pl.semaphore_wait(barrier, len(offsets))
    own = pltpu.make_async_copy(stats_ref.at[0, 0], out_ref.at[0, 0, 0], own_sem)
    own.start()
    cps = []
    for k, (dx, dz, dy) in enumerate(offsets):
        cp = pltpu.make_async_remote_copy(
            src_ref=stats_ref.at[dz, dx],
            dst_ref=out_ref.at[(n_tp - dy) % n_tp, (4 - dz) % 4, (4 - dx) % 4],
            send_sem=send_sems.at[k],
            recv_sem=recv_sems.at[k],
            device_id=peer(dx, dz, dy),
            device_id_type=MESH,
        )
        cp.start()
        cps.append(cp)
    own.wait()
    for cp in cps:
        cp.wait()


def exchange_all(stats, n_tp):
    n = n_tp * 16 - 1
    return pl.pallas_call(
        functools.partial(plane_kernel, n_tp),
        out_shape=jax.ShapeDtypeStruct((n_tp, *stats.shape), stats.dtype),
        in_specs=[pl.BlockSpec(memory_space=pl.ANY)],
        out_specs=pl.BlockSpec(memory_space=pl.ANY),
        scratch_shapes=[
            pltpu.SemaphoreType.DMA,
            pltpu.SemaphoreType.DMA((n,)),
            pltpu.SemaphoreType.DMA((n,)),
        ],
        compiler_params=pltpu.CompilerParams(collective_id=2, has_side_effects=True),
    )(stats)


def per_device(hidden_states, norm_gain, head, target_ids, lengths):
    feats = hidden_states.astype(jnp.float32)
    scale = lax.rsqrt(jnp.mean(feats * feats, axis=-1, keepdims=True) + 1e-06)
    normed = (feats * scale * norm_gain).astype(jnp.bfloat16)
    rows, dim = normed.shape
    vdev = head.shape[1]
    n_tp = lax.axis_size("tp")
    xi = lax.axis_index("x")
    zi = lax.axis_index("z")
    core = lax.axis_index("core")
    tp = lax.axis_index("tp")
    n_z = lax.axis_size("z")
    chip = xi * n_z + zi
    piece = normed
    head_t = head.T
    tin = jnp.broadcast_to(target_ids.astype(jnp.float32).reshape(2, 1, rows // 2), (2, 8, rows // 2))
    _, stats = gather_and_stats(piece, head_t, tin, n_tp)
    h = rows // 2
    order = jnp.array([0, 3, 2, 1])
    st = stats[:, :4].reshape(4, 2, 4, 4, h)
    s_a = jnp.transpose(st[:, 0], (1, 0, 2, 3))[:, order]
    s_b = jnp.transpose(st[:, 1], (1, 2, 0, 3))[:, :, order]
    rel = jnp.concatenate([s_a, s_b], axis=3)
    arrived = exchange_all(jnp.moveaxis(rel, 0, 2), n_tp)
    arrived = jnp.roll(arrived, tp, axis=0)
    top, weight_sum, weighted, picked = merge(arrived.reshape(-1, 4, rows), axis=0)
    log_norm = top + jnp.log(weight_sum)
    live = jnp.arange(rows, dtype=jnp.int32) < lengths[0]
    logprob = jnp.where(live, picked - log_norm, jnp.float32(0.0))
    entropy = jnp.where(live, log_norm - weighted / weight_sum, jnp.float32(0.0))
    mean_lp = (jnp.sum(logprob) / lengths[0].astype(jnp.float32)).reshape(1)
    top_live = jnp.max(jnp.where(live, top, jnp.float32(-1e30))).reshape(1)
    return (logprob, entropy, mean_lp, top_live)


def solution(mesh):
    n_req, n_tp = mesh.devices.shape
    devices = np.asarray(mesh.devices).reshape(4, n_req // 8, 2, n_tp)
    fine = Mesh(devices, ("x", "z", "core", "tp"))
    rq = ("x", "z", "core")
    in_specs = (P(rq, None), P(), P(None, (*rq, "tp")), P(rq), P(rq))
    out_specs = (P(rq), P(rq), P(rq), P(rq))
    return jax.shard_map(
        per_device, mesh=fine, in_specs=in_specs, out_specs=out_specs, check_vma=False
    )
```

```python
import functools

import jax
import jax.numpy as jnp
import numpy as np
from jax import lax
from jax.experimental import pallas as pl
from jax.experimental.pallas import tpu as pltpu
from jax.sharding import Mesh, PartitionSpec as P

MESH = pl.DeviceIdType.MESH
EXTRA = 128


def slice_stats(block, target, matrix, vocab_ids):
    logits = jnp.dot(block, matrix, preferred_element_type=jnp.float32)
    top = jnp.max(logits, axis=-1)
    shifted = jnp.exp(logits - top[:, None])
    weight_sum = jnp.sum(shifted, axis=-1)
    weighted = jnp.sum(shifted * logits, axis=-1)
    hit = vocab_ids == target[:, None]
    picked = jnp.sum(jnp.where(hit, logits, 0.0), axis=-1)
    return jnp.stack([top, weight_sum, weighted, picked])


def merge(stats, axis):
    top = jnp.max(stats[:, 0], axis=axis)
    factor = jnp.exp(stats[:, 0] - jnp.expand_dims(top, axis))
    return (
        top,
        jnp.sum(stats[:, 1] * factor, axis=axis),
        jnp.sum(stats[:, 2] * factor, axis=axis),
        jnp.sum(stats[:, 3], axis=axis),
    )


def fused_kernel(n_tp, piece_ref, head_ref, tin_ref, out_ref, stats_ref,
                 hboth, raw, vbuf, tgt, local_sems, head_sems, send_sems, recv_sems, load_sems):
    xi, zi = lax.axis_index("x"), lax.axis_index("z")
    core, tp = lax.axis_index("core"), lax.axis_index("tp")
    vdev = head_ref.shape[1]

    def dev(dx, dz):
        return (lax.rem(xi + dx, 4), lax.rem(zi + dz, 4), core, tp)

    partner = (xi, zi, 1 - core, tp)
    barrier = pltpu.get_barrier_semaphore()
    for dx, dz in ((1, 0), (3, 0), (0, 1), (0, 3)):
        pl.semaphore_signal(barrier, inc=1, device_id=dev(dx, dz), device_id_type=MESH)
    pl.semaphore_signal(barrier, inc=1, device_id=partner, device_id_type=MESH)
    pl.semaphore_wait(barrier, 5)
    mine = pl.ds(pl.multiple_of(core * vdev, vdev), vdev)
    theirs = pl.ds(pl.multiple_of((1 - core) * vdev, vdev), vdev)
    swap = pltpu.make_async_remote_copy(
        src_ref=head_ref,
        dst_ref=raw.at[1],
        send_sem=head_sems.at[0],
        recv_sem=head_sems.at[1],
        device_id=partner,
        device_id_type=MESH,
    )
    swap.start()
    own_head = pltpu.make_async_copy(head_ref, raw.at[0], local_sems.at[0])
    own_head.start()
    sel = pltpu.make_async_copy(tin_ref, tgt.at[0, 0], local_sems.at[1])
    sel.start()
    own = pltpu.make_async_copy(piece_ref, out_ref.at[0, 0], local_sems.at[2])
    own.start()
    rows = piece_ref.shape[0]
    h, q = rows // 2, rows // 4
    count = [0]

    def send(src, dst, dx, dz):
        k = count[0]
        count[0] += 1
        cp = pltpu.make_async_remote_copy(
            src_ref=src,
            dst_ref=dst,
            send_sem=send_sems.at[k],
            recv_sem=recv_sems.at[k],
            device_id=dev(dx, dz),
            device_id_type=MESH,
        )
        cp.start()
        return cp

    def finish(cps):
        for cp in cps:
            cp.wait()

    chip = xi * 4 + zi
    ids = lax.broadcasted_iota(jnp.int32, (2 * vdev, 1), 0)
    vocab = (((chip * 2 + ids // vdev) * n_tp + tp) * vdev + ids % vdev).astype(jnp.float32)

    def group(m, half):
        off = lax.rem(m * 3, 4)
        loads = []
        for j in range(4):
            if half == 0:
                src = out_ref.at[off, j, pl.ds(0, h)]
            else:
                src = out_ref.at[j, off, pl.ds(h, h)]
            cp = pltpu.make_async_copy(src, vbuf.at[j], load_sems.at[j])
            cp.start()
            loads.append(cp)
        finish(loads)
        block = vbuf[...].reshape(4 * h, vbuf.shape[2])
        real = lax.dot_general(
            hboth[...], block, (((1,), (1,)), ((), ())), preferred_element_type=jnp.float32
        )
        if half == 0:
            pieces = [tgt[off, j, 0, 0:1, :] for j in range(4)]
        else:
            pieces = [tgt[j, off, 1, 0:1, :] for j in range(4)]
        target = jnp.concatenate(pieces, axis=1)
        top = jnp.max(real, axis=0, keepdims=True)
        shifted = jnp.exp(real - top)
        g = m * 2 + half
        stats_ref[g, 0:1, :] = top
        stats_ref[g, 1:2, :] = jnp.sum(shifted, axis=0, keepdims=True)
        stats_ref[g, 2:3, :] = jnp.sum(shifted * real, axis=0, keepdims=True)
        stats_ref[g, 3:4, :] = jnp.sum(jnp.where(vocab == target, real, 0.0), axis=0, keepdims=True)

    def phase(ms):
        def body(i, carry):
            m = ms[0] + i * (ms[1] - ms[0]) if len(ms) > 1 else ms[0] + i * 0
            group(m, 0)
            group(m, 1)
            return carry

        lax.fori_loop(0, len(ms), body, 0)

    first = [
        send(piece_ref.at[0:h], out_ref.at[0, 3, 0:h], 1, 0),
        send(piece_ref.at[0:h], out_ref.at[0, 1, 0:h], 3, 0),
        send(piece_ref.at[h:rows], out_ref.at[3, 0, h:rows], 0, 1),
        send(piece_ref.at[h:rows], out_ref.at[1, 0, h:rows], 0, 3),
        send(tin_ref.at[0], tgt.at[0, 3, 0], 1, 0),
        send(tin_ref.at[0], tgt.at[0, 1, 0], 3, 0),
        send(tin_ref.at[1], tgt.at[3, 0, 1], 0, 1),
        send(tin_ref.at[1], tgt.at[1, 0, 1], 0, 3),
    ]
    own_head.wait()
    hboth[mine] = raw[0].T
    finish(first)
    second = [
        send(out_ref.at[0, 3, 0:q], out_ref.at[0, 2, 0:q], 1, 0),
        send(out_ref.at[0, 1, q:h], out_ref.at[0, 2, q:h], 3, 0),
        send(out_ref.at[3, 0, h:h + q], out_ref.at[2, 0, h:h + q], 0, 1),
        send(out_ref.at[1, 0, h + q:rows], out_ref.at[2, 0, h + q:rows], 0, 3),
        send(tgt.at[0, 3, 0], tgt.at[0, 2, 0], 1, 0),
        send(tgt.at[3, 0, 1], tgt.at[2, 0, 1], 0, 1),
    ]
    swap.wait()
    hboth[theirs] = raw[1].T
    finish(second)
    own.wait()
    sel.wait()
    third = [
        send(out_ref.at[0, :, 0:h], out_ref.at[3, :, 0:h], 0, 1),
        send(out_ref.at[0, :, 0:h], out_ref.at[1, :, 0:h], 0, 3),
        send(out_ref.at[:, 0, h:rows], out_ref.at[:, 3, h:rows], 1, 0),
        send(out_ref.at[:, 0, h:rows], out_ref.at[:, 1, h:rows], 3, 0),
        send(tgt.at[0, :, 0], tgt.at[3, :, 0], 0, 1),
        send(tgt.at[0, :, 0], tgt.at[1, :, 0], 0, 3),
        send(tgt.at[:, 0, 1], tgt.at[:, 3, 1], 1, 0),
        send(tgt.at[:, 0, 1], tgt.at[:, 1, 1], 3, 0),
    ]
    phase((0,))
    finish(third)
    fourth = [
        send(out_ref.at[3, :, 0:q], out_ref.at[2, :, 0:q], 0, 1),
        send(out_ref.at[1, :, q:h], out_ref.at[2, :, q:h], 0, 3),
        send(out_ref.at[:, 3, h:h + q], out_ref.at[:, 2, h:h + q], 1, 0),
        send(out_ref.at[:, 1, h + q:rows], out_ref.at[:, 2, h + q:rows], 3, 0),
        send(tgt.at[3, :, 0], tgt.at[2, :, 0], 0, 1),
        send(tgt.at[:, 3, 1], tgt.at[:, 2, 1], 1, 0),
    ]
    phase((1, 3))
    finish(fourth)
    phase((2,))


def gather_and_stats(piece, head_t, tin, n_tp):
    rows, cols = piece.shape
    vdev = head_t.shape[1]
    h = rows // 2
    return pl.pallas_call(
        functools.partial(fused_kernel, n_tp),
        out_shape=(
            jax.ShapeDtypeStruct((4, 4, rows, cols), piece.dtype),
            jax.ShapeDtypeStruct((8, 8, 4 * h), jnp.float32),
        ),
        in_specs=[pl.BlockSpec(memory_space=pl.ANY)] * 3,
        out_specs=(pl.BlockSpec(memory_space=pl.ANY), pl.BlockSpec(memory_space=pltpu.VMEM)),
        scratch_shapes=[
            pltpu.VMEM((2 * vdev, cols), jnp.bfloat16),
            pltpu.VMEM((2, cols, vdev), jnp.bfloat16),
            pltpu.VMEM((4, h, cols), jnp.bfloat16),
            pltpu.VMEM((4, 4, 2, 8, h), jnp.float32),
            pltpu.SemaphoreType.DMA((3,)),
            pltpu.SemaphoreType.DMA((2,)),
            pltpu.SemaphoreType.DMA((28,)),
            pltpu.SemaphoreType.DMA((28,)),
            pltpu.SemaphoreType.DMA((4,)),
        ],
        compiler_params=pltpu.CompilerParams(
            collective_id=1, has_side_effects=True, vmem_limit_bytes=60 * 1024 * 1024
        ),
    )(piece, head_t, tin)


def plane_kernel(n_tp, stats_ref, out_ref, own_sem, send_sems, recv_sems):
    xi, zi = lax.axis_index("x"), lax.axis_index("z")
    core, tp = lax.axis_index("core"), lax.axis_index("tp")
    offsets = [(dx, dz, dy) for dy in range(n_tp) for dz in range(4) for dx in range(4) if dx or dz or dy]

    def peer(dx, dz, dy):
        return (lax.rem(xi + dx, 4), lax.rem(zi + dz, 4), core, lax.rem(tp + dy, n_tp))

    barrier = pltpu.get_barrier_semaphore()
    for dx, dz, dy in offsets:
        pl.semaphore_signal(barrier, inc=1, device_id=peer(dx, dz, dy), device_id_type=MESH)
    pl.semaphore_wait(barrier, len(offsets))
    own = pltpu.make_async_copy(stats_ref.at[0, 0], out_ref.at[0, 0, 0], own_sem)
    own.start()
    cps = []
    for k, (dx, dz, dy) in enumerate(offsets):
        cp = pltpu.make_async_remote_copy(
            src_ref=stats_ref.at[dz, dx],
            dst_ref=out_ref.at[(n_tp - dy) % n_tp, (4 - dz) % 4, (4 - dx) % 4],
            send_sem=send_sems.at[k],
            recv_sem=recv_sems.at[k],
            device_id=peer(dx, dz, dy),
            device_id_type=MESH,
        )
        cp.start()
        cps.append(cp)
    own.wait()
    for cp in cps:
        cp.wait()


def exchange_all(stats, n_tp):
    n = n_tp * 16 - 1
    return pl.pallas_call(
        functools.partial(plane_kernel, n_tp),
        out_shape=jax.ShapeDtypeStruct((n_tp, *stats.shape), stats.dtype),
        in_specs=[pl.BlockSpec(memory_space=pl.ANY)],
        out_specs=pl.BlockSpec(memory_space=pl.ANY),
        scratch_shapes=[
            pltpu.SemaphoreType.DMA,
            pltpu.SemaphoreType.DMA((n,)),
            pltpu.SemaphoreType.DMA((n,)),
        ],
        compiler_params=pltpu.CompilerParams(collective_id=2, has_side_effects=True),
    )(stats)


def per_device(hidden_states, norm_gain, head, target_ids, lengths):
    feats = hidden_states.astype(jnp.float32)
    scale = lax.rsqrt(jnp.mean(feats * feats, axis=-1, keepdims=True) + 1e-06)
    normed = (feats * scale * norm_gain).astype(jnp.bfloat16)
    rows, dim = normed.shape
    vdev = head.shape[1]
    n_tp = lax.axis_size("tp")
    xi = lax.axis_index("x")
    zi = lax.axis_index("z")
    core = lax.axis_index("core")
    tp = lax.axis_index("tp")
    n_z = lax.axis_size("z")
    chip = xi * n_z + zi
    piece = normed
    head_t = head
    tin = jnp.broadcast_to(target_ids.astype(jnp.float32).reshape(2, 1, rows // 2), (2, 8, rows // 2))
    _, stats = gather_and_stats(piece, head_t, tin, n_tp)
    h = rows // 2
    order = jnp.array([0, 3, 2, 1])
    st = stats[:, :4].reshape(4, 2, 4, 4, h)
    s_a = jnp.transpose(st[:, 0], (1, 0, 2, 3))[:, order]
    s_b = jnp.transpose(st[:, 1], (1, 2, 0, 3))[:, :, order]
    rel = jnp.concatenate([s_a, s_b], axis=3)
    arrived = exchange_all(jnp.moveaxis(rel, 0, 2), n_tp)
    arrived = jnp.roll(arrived, tp, axis=0)
    top, weight_sum, weighted, picked = merge(arrived.reshape(-1, 4, rows), axis=0)
    log_norm = top + jnp.log(weight_sum)
    live = jnp.arange(rows, dtype=jnp.int32) < lengths[0]
    logprob = jnp.where(live, picked - log_norm, jnp.float32(0.0))
    entropy = jnp.where(live, log_norm - weighted / weight_sum, jnp.float32(0.0))
    mean_lp = (jnp.sum(logprob) / lengths[0].astype(jnp.float32)).reshape(1)
    top_live = jnp.max(jnp.where(live, top, jnp.float32(-1e30))).reshape(1)
    return (logprob, entropy, mean_lp, top_live)


def solution(mesh):
    n_req, n_tp = mesh.devices.shape
    devices = np.asarray(mesh.devices).reshape(4, n_req // 8, 2, n_tp)
    fine = Mesh(devices, ("x", "z", "core", "tp"))
    rq = ("x", "z", "core")
    in_specs = (P(rq, None), P(), P(None, (*rq, "tp")), P(rq), P(rq))
    out_specs = (P(rq), P(rq), P(rq), P(rq))
    return jax.shard_map(
        per_device, mesh=fine, in_specs=in_specs, out_specs=out_specs, check_vma=False
    )
```

```python
import functools

import jax
import jax.numpy as jnp
import numpy as np
from jax import lax
from jax.experimental import pallas as pl
from jax.experimental.pallas import tpu as pltpu
from jax.sharding import Mesh, PartitionSpec as P

MESH = pl.DeviceIdType.MESH
EXTRA = 128


def slice_stats(block, target, matrix, vocab_ids):
    logits = jnp.dot(block, matrix, preferred_element_type=jnp.float32)
    top = jnp.max(logits, axis=-1)
    shifted = jnp.exp(logits - top[:, None])
    weight_sum = jnp.sum(shifted, axis=-1)
    weighted = jnp.sum(shifted * logits, axis=-1)
    hit = vocab_ids == target[:, None]
    picked = jnp.sum(jnp.where(hit, logits, 0.0), axis=-1)
    return jnp.stack([top, weight_sum, weighted, picked])


def merge(stats, axis):
    top = jnp.max(stats[:, 0], axis=axis)
    factor = jnp.exp(stats[:, 0] - jnp.expand_dims(top, axis))
    return (
        top,
        jnp.sum(stats[:, 1] * factor, axis=axis),
        jnp.sum(stats[:, 2] * factor, axis=axis),
        jnp.sum(stats[:, 3], axis=axis),
    )


def fused_kernel(n_tp, piece_ref, head_ref, tin_ref, out_ref, stats_ref,
                 hboth, raw, vbuf, tgt, local_sems, head_sems, send_sems, recv_sems, load_sems):
    xi, zi = lax.axis_index("x"), lax.axis_index("z")
    core, tp = lax.axis_index("core"), lax.axis_index("tp")
    vdev = head_ref.shape[1]

    def dev(dx, dz):
        return (lax.rem(xi + dx, 4), lax.rem(zi + dz, 4), core, tp)

    partner = (xi, zi, 1 - core, tp)
    barrier = pltpu.get_barrier_semaphore()
    for dx, dz in ((1, 0), (3, 0), (0, 1), (0, 3)):
        pl.semaphore_signal(barrier, inc=1, device_id=dev(dx, dz), device_id_type=MESH)
    pl.semaphore_signal(barrier, inc=1, device_id=partner, device_id_type=MESH)
    pl.semaphore_wait(barrier, 5)
    mine = pl.ds(pl.multiple_of(core * vdev, vdev), vdev)
    theirs = pl.ds(pl.multiple_of((1 - core) * vdev, vdev), vdev)
    swap = pltpu.make_async_remote_copy(
        src_ref=head_ref,
        dst_ref=raw.at[1],
        send_sem=head_sems.at[0],
        recv_sem=head_sems.at[1],
        device_id=partner,
        device_id_type=MESH,
    )
    swap.start()
    own_head = pltpu.make_async_copy(head_ref, raw.at[0], local_sems.at[0])
    own_head.start()
    sel = pltpu.make_async_copy(tin_ref, tgt.at[0, 0], local_sems.at[1])
    sel.start()
    own = pltpu.make_async_copy(piece_ref, out_ref.at[0, 0], local_sems.at[2])
    own.start()
    rows = piece_ref.shape[0]
    h, q = rows // 2, rows // 4
    count = [0]

    def send(src, dst, dx, dz):
        k = count[0]
        count[0] += 1
        cp = pltpu.make_async_remote_copy(
            src_ref=src,
            dst_ref=dst,
            send_sem=send_sems.at[k],
            recv_sem=recv_sems.at[k],
            device_id=dev(dx, dz),
            device_id_type=MESH,
        )
        cp.start()
        return cp

    def finish(cps):
        for cp in cps:
            cp.wait()

    chip = xi * 4 + zi
    ids = lax.broadcasted_iota(jnp.int32, (2 * vdev, 1), 0)
    vocab = (((chip * 2 + ids // vdev) * n_tp + tp) * vdev + ids % vdev).astype(jnp.float32)

    def group(m, half):
        off = lax.rem(m * 3, 4)
        loads = []
        for j in range(4):
            if half == 0:
                src = out_ref.at[off, j, pl.ds(0, h)]
            else:
                src = out_ref.at[j, off, pl.ds(h, h)]
            cp = pltpu.make_async_copy(src, vbuf.at[j], load_sems.at[j])
            cp.start()
            loads.append(cp)
        finish(loads)
        block = vbuf[...].reshape(4 * h, vbuf.shape[2])
        real = lax.dot_general(
            hboth[...], block, (((1,), (1,)), ((), ())), preferred_element_type=jnp.float32
        )
        if half == 0:
            pieces = [tgt[off, j, 0, 0:1, :] for j in range(4)]
        else:
            pieces = [tgt[j, off, 1, 0:1, :] for j in range(4)]
        target = jnp.concatenate(pieces, axis=1)
        top = jnp.max(real, axis=0, keepdims=True)
        shifted = jnp.exp(real - top)
        g = m * 2 + half
        stats_ref[g, 0:1, :] = top
        stats_ref[g, 1:2, :] = jnp.sum(shifted, axis=0, keepdims=True)
        stats_ref[g, 2:3, :] = jnp.sum(shifted * real, axis=0, keepdims=True)
        stats_ref[g, 3:4, :] = jnp.sum(jnp.where(vocab == target, real, 0.0), axis=0, keepdims=True)

    def phase(ms):
        def body(i, carry):
            m = ms[0] + i * (ms[1] - ms[0]) if len(ms) > 1 else ms[0] + i * 0
            group(m, 0)
            group(m, 1)
            return carry

        lax.fori_loop(0, len(ms), body, 0)

    first = [
        send(piece_ref.at[0:h], out_ref.at[0, 3, 0:h], 1, 0),
        send(piece_ref.at[0:h], out_ref.at[0, 1, 0:h], 3, 0),
        send(piece_ref.at[h:rows], out_ref.at[3, 0, h:rows], 0, 1),
        send(piece_ref.at[h:rows], out_ref.at[1, 0, h:rows], 0, 3),
        send(tin_ref.at[0], tgt.at[0, 3, 0], 1, 0),
        send(tin_ref.at[0], tgt.at[0, 1, 0], 3, 0),
        send(tin_ref.at[1], tgt.at[3, 0, 1], 0, 1),
        send(tin_ref.at[1], tgt.at[1, 0, 1], 0, 3),
    ]
    own_head.wait()
    hboth[mine] = raw[0].T
    finish(first)
    second = [
        send(out_ref.at[0, 3, 0:q], out_ref.at[0, 2, 0:q], 1, 0),
        send(out_ref.at[0, 1, q:h], out_ref.at[0, 2, q:h], 3, 0),
        send(out_ref.at[3, 0, h:h + q], out_ref.at[2, 0, h:h + q], 0, 1),
        send(out_ref.at[1, 0, h + q:rows], out_ref.at[2, 0, h + q:rows], 0, 3),
        send(tgt.at[0, 3, 0], tgt.at[0, 2, 0], 1, 0),
        send(tgt.at[3, 0, 1], tgt.at[2, 0, 1], 0, 1),
    ]
    swap.wait()
    hboth[theirs] = raw[1].T
    finish(second)
    own.wait()
    sel.wait()
    third = [
        send(out_ref.at[0, :, 0:h], out_ref.at[3, :, 0:h], 0, 1),
        send(out_ref.at[0, :, 0:h], out_ref.at[1, :, 0:h], 0, 3),
        send(out_ref.at[:, 0, h:rows], out_ref.at[:, 3, h:rows], 1, 0),
        send(out_ref.at[:, 0, h:rows], out_ref.at[:, 1, h:rows], 3, 0),
        send(tgt.at[0, :, 0], tgt.at[3, :, 0], 0, 1),
        send(tgt.at[0, :, 0], tgt.at[1, :, 0], 0, 3),
        send(tgt.at[:, 0, 1], tgt.at[:, 3, 1], 1, 0),
        send(tgt.at[:, 0, 1], tgt.at[:, 1, 1], 3, 0),
    ]
    phase((0,))
    finish(third)
    fourth = [
        send(out_ref.at[3, :, 0:q], out_ref.at[2, :, 0:q], 0, 1),
        send(out_ref.at[1, :, q:h], out_ref.at[2, :, q:h], 0, 3),
        send(out_ref.at[:, 3, h:h + q], out_ref.at[:, 2, h:h + q], 1, 0),
        send(out_ref.at[:, 1, h + q:rows], out_ref.at[:, 2, h + q:rows], 3, 0),
        send(tgt.at[3, :, 0], tgt.at[2, :, 0], 0, 1),
        send(tgt.at[:, 3, 1], tgt.at[:, 2, 1], 1, 0),
    ]
    phase((1, 3))
    finish(fourth)
    phase((2,))


def gather_and_stats(piece, head_t, tin, n_tp):
    rows, cols = piece.shape
    vdev = head_t.shape[1]
    h = rows // 2
    return pl.pallas_call(
        functools.partial(fused_kernel, n_tp),
        out_shape=(
            jax.ShapeDtypeStruct((4, 4, rows, cols), piece.dtype),
            jax.ShapeDtypeStruct((8, 8, 4 * h), jnp.float32),
        ),
        in_specs=[pl.BlockSpec(memory_space=pl.ANY)] * 3,
        out_specs=(pl.BlockSpec(memory_space=pl.ANY), pl.BlockSpec(memory_space=pltpu.VMEM)),
        scratch_shapes=[
            pltpu.VMEM((2 * vdev, cols), jnp.bfloat16),
            pltpu.VMEM((2, cols, vdev), jnp.bfloat16),
            pltpu.VMEM((4, h, cols), jnp.bfloat16),
            pltpu.VMEM((4, 4, 2, 8, h), jnp.float32),
            pltpu.SemaphoreType.DMA((3,)),
            pltpu.SemaphoreType.DMA((2,)),
            pltpu.SemaphoreType.DMA((28,)),
            pltpu.SemaphoreType.DMA((28,)),
            pltpu.SemaphoreType.DMA((4,)),
        ],
        compiler_params=pltpu.CompilerParams(
            collective_id=1, has_side_effects=True, vmem_limit_bytes=60 * 1024 * 1024
        ),
    )(piece, head_t, tin)


def plane_kernel(n_tp, stats_ref, out_ref, own_sem, send_sems, recv_sems):
    xi, zi = lax.axis_index("x"), lax.axis_index("z")
    core, tp = lax.axis_index("core"), lax.axis_index("tp")
    offsets = [(dx, dz, dy) for dy in range(n_tp) for dz in range(4) for dx in range(4) if dx or dz or dy]

    def peer(dx, dz, dy):
        return (lax.rem(xi + dx, 4), lax.rem(zi + dz, 4), core, lax.rem(tp + dy, n_tp))

    barrier = pltpu.get_barrier_semaphore()
    for dx, dz, dy in offsets:
        pl.semaphore_signal(barrier, inc=1, device_id=peer(dx, dz, dy), device_id_type=MESH)
    pl.semaphore_wait(barrier, len(offsets))
    own = pltpu.make_async_copy(stats_ref.at[0, 0], out_ref.at[0, 0, 0], own_sem)
    own.start()
    cps = []
    for k, (dx, dz, dy) in enumerate(offsets):
        cp = pltpu.make_async_remote_copy(
            src_ref=stats_ref.at[dz, dx],
            dst_ref=out_ref.at[(n_tp - dy) % n_tp, (4 - dz) % 4, (4 - dx) % 4],
            send_sem=send_sems.at[k],
            recv_sem=recv_sems.at[k],
            device_id=peer(dx, dz, dy),
            device_id_type=MESH,
        )
        cp.start()
        cps.append(cp)
    own.wait()
    for cp in cps:
        cp.wait()


def exchange_all(stats, n_tp):
    n = n_tp * 16 - 1
    return pl.pallas_call(
        functools.partial(plane_kernel, n_tp),
        out_shape=jax.ShapeDtypeStruct((n_tp, *stats.shape), stats.dtype),
        in_specs=[pl.BlockSpec(memory_space=pl.ANY)],
        out_specs=pl.BlockSpec(memory_space=pl.ANY),
        scratch_shapes=[
            pltpu.SemaphoreType.DMA,
            pltpu.SemaphoreType.DMA((n,)),
            pltpu.SemaphoreType.DMA((n,)),
        ],
        compiler_params=pltpu.CompilerParams(collective_id=2, has_side_effects=True),
    )(stats)


def per_device(hidden_states, norm_gain, head, target_ids, lengths):
    feats = hidden_states.astype(jnp.float32)
    scale = lax.rsqrt(jnp.mean(feats * feats, axis=-1, keepdims=True) + 1e-06)
    normed = (feats * scale * norm_gain).astype(jnp.bfloat16)
    rows, dim = normed.shape
    vdev = head.shape[1]
    n_tp = lax.axis_size("tp")
    xi = lax.axis_index("x")
    zi = lax.axis_index("z")
    core = lax.axis_index("core")
    tp = lax.axis_index("tp")
    n_z = lax.axis_size("z")
    chip = xi * n_z + zi
    piece = normed
    head_t = head
    tin = jnp.broadcast_to(target_ids.astype(jnp.float32).reshape(2, 1, rows // 2), (2, 8, rows // 2))
    _, stats = gather_and_stats(piece, head_t, tin, n_tp)
    h = rows // 2
    st = stats[:, :4].reshape(4, 2, 4, 4, h)
    by_offset = jnp.stack([st[0], st[3], st[2], st[1]])
    s_a = jnp.transpose(by_offset[:, 0], (1, 0, 2, 3))
    s_b = jnp.transpose(by_offset[:, 1], (1, 2, 0, 3))
    rel = jnp.concatenate([s_a, s_b], axis=3)
    arrived = exchange_all(jnp.moveaxis(rel, 0, 2), n_tp)
    arrived = jnp.roll(arrived, tp, axis=0)
    top, weight_sum, weighted, picked = merge(arrived.reshape(-1, 4, rows), axis=0)
    log_norm = top + jnp.log(weight_sum)
    live = jnp.arange(rows, dtype=jnp.int32) < lengths[0]
    logprob = jnp.where(live, picked - log_norm, jnp.float32(0.0))
    entropy = jnp.where(live, log_norm - weighted / weight_sum, jnp.float32(0.0))
    mean_lp = (jnp.sum(logprob) / lengths[0].astype(jnp.float32)).reshape(1)
    top_live = jnp.max(jnp.where(live, top, jnp.float32(-1e30))).reshape(1)
    return (logprob, entropy, mean_lp, top_live)


def solution(mesh):
    n_req, n_tp = mesh.devices.shape
    devices = np.asarray(mesh.devices).reshape(4, n_req // 8, 2, n_tp)
    fine = Mesh(devices, ("x", "z", "core", "tp"))
    rq = ("x", "z", "core")
    in_specs = (P(rq, None), P(), P(None, (*rq, "tp")), P(rq), P(rq))
    out_specs = (P(rq), P(rq), P(rq), P(rq))
    return jax.shard_map(
        per_device, mesh=fine, in_specs=in_specs, out_specs=out_specs, check_vma=False
    )
```

```python
import functools

import jax
import jax.numpy as jnp
import numpy as np
from jax import lax
from jax.experimental import pallas as pl
from jax.experimental.pallas import tpu as pltpu
from jax.sharding import Mesh, PartitionSpec as P

MESH = pl.DeviceIdType.MESH
EXTRA = 128


def slice_stats(block, target, matrix, vocab_ids):
    logits = jnp.dot(block, matrix, preferred_element_type=jnp.float32)
    top = jnp.max(logits, axis=-1)
    shifted = jnp.exp(logits - top[:, None])
    weight_sum = jnp.sum(shifted, axis=-1)
    weighted = jnp.sum(shifted * logits, axis=-1)
    hit = vocab_ids == target[:, None]
    picked = jnp.sum(jnp.where(hit, logits, 0.0), axis=-1)
    return jnp.stack([top, weight_sum, weighted, picked])


def merge(stats, axis):
    top = jnp.max(stats[:, 0], axis=axis)
    factor = jnp.exp(stats[:, 0] - jnp.expand_dims(top, axis))
    return (
        top,
        jnp.sum(stats[:, 1] * factor, axis=axis),
        jnp.sum(stats[:, 2] * factor, axis=axis),
        jnp.sum(stats[:, 3], axis=axis),
    )


def fused_kernel(n_tp, piece_ref, head_ref, tin_ref, out_ref, stats_ref,
                 hboth, raw, vbuf, tgt, local_sems, head_sems, send_sems, recv_sems, load_sems):
    xi, zi = lax.axis_index("x"), lax.axis_index("z")
    core, tp = lax.axis_index("core"), lax.axis_index("tp")
    vdev = head_ref.shape[1]

    def dev(dx, dz):
        return (lax.rem(xi + dx, 4), lax.rem(zi + dz, 4), core, tp)

    partner = (xi, zi, 1 - core, tp)
    barrier = pltpu.get_barrier_semaphore()
    for dx, dz in ((1, 0), (3, 0), (0, 1), (0, 3)):
        pl.semaphore_signal(barrier, inc=1, device_id=dev(dx, dz), device_id_type=MESH)
    pl.semaphore_signal(barrier, inc=1, device_id=partner, device_id_type=MESH)
    pl.semaphore_wait(barrier, 5)
    mine = pl.ds(pl.multiple_of(core * vdev, vdev), vdev)
    theirs = pl.ds(pl.multiple_of((1 - core) * vdev, vdev), vdev)
    swap = pltpu.make_async_remote_copy(
        src_ref=head_ref,
        dst_ref=raw.at[1],
        send_sem=head_sems.at[0],
        recv_sem=head_sems.at[1],
        device_id=partner,
        device_id_type=MESH,
    )
    swap.start()
    own_head = pltpu.make_async_copy(head_ref, raw.at[0], local_sems.at[0])
    own_head.start()
    sel = pltpu.make_async_copy(tin_ref, tgt.at[0, 0], local_sems.at[1])
    sel.start()
    own = pltpu.make_async_copy(piece_ref, out_ref.at[0, 0], local_sems.at[2])
    own.start()
    rows = piece_ref.shape[0]
    h, q = rows // 2, rows // 4
    count = [0]

    def send(src, dst, dx, dz):
        k = count[0]
        count[0] += 1
        cp = pltpu.make_async_remote_copy(
            src_ref=src,
            dst_ref=dst,
            send_sem=send_sems.at[k],
            recv_sem=recv_sems.at[k],
            device_id=dev(dx, dz),
            device_id_type=MESH,
        )
        cp.start()
        return cp

    def finish(cps):
        for cp in cps:
            cp.wait()

    chip = xi * 4 + zi
    ids = lax.broadcasted_iota(jnp.int32, (2 * vdev, 1), 0)
    vocab = (((chip * 2 + ids // vdev) * n_tp + tp) * vdev + ids % vdev).astype(jnp.float32)

    def group(m, half):
        off = lax.rem(m * 3, 4)
        loads = []
        for j in range(4):
            if half == 0:
                src = out_ref.at[off, j, pl.ds(0, h)]
            else:
                src = out_ref.at[j, off, pl.ds(h, h)]
            cp = pltpu.make_async_copy(src, vbuf.at[j], load_sems.at[j])
            cp.start()
            loads.append(cp)
        finish(loads)
        block = vbuf[...].reshape(4 * h, vbuf.shape[2])
        real = lax.dot_general(
            hboth[...], block, (((1,), (1,)), ((), ())), preferred_element_type=jnp.float32
        )
        if half == 0:
            pieces = [tgt[off, j, 0, 0:1, :] for j in range(4)]
        else:
            pieces = [tgt[j, off, 1, 0:1, :] for j in range(4)]
        target = jnp.concatenate(pieces, axis=1)
        top = jnp.max(real, axis=0, keepdims=True)
        shifted = jnp.exp(real - top)
        g = m * 2 + half
        stats_ref[g, 0:1, :] = top
        stats_ref[g, 1:2, :] = jnp.sum(shifted, axis=0, keepdims=True)
        stats_ref[g, 2:3, :] = jnp.sum(shifted * real, axis=0, keepdims=True)
        stats_ref[g, 3:4, :] = jnp.sum(jnp.where(vocab == target, real, 0.0), axis=0, keepdims=True)

    def phase(ms):
        def body(i, carry):
            m = ms[0] + i * (ms[1] - ms[0]) if len(ms) > 1 else ms[0] + i * 0
            group(m, 0)
            group(m, 1)
            return carry

        lax.fori_loop(0, len(ms), body, 0)

    first = [
        send(piece_ref.at[0:h], out_ref.at[0, 3, 0:h], 1, 0),
        send(piece_ref.at[0:h], out_ref.at[0, 1, 0:h], 3, 0),
        send(piece_ref.at[h:rows], out_ref.at[3, 0, h:rows], 0, 1),
        send(piece_ref.at[h:rows], out_ref.at[1, 0, h:rows], 0, 3),
        send(tin_ref.at[0], tgt.at[0, 3, 0], 1, 0),
        send(tin_ref.at[0], tgt.at[0, 1, 0], 3, 0),
        send(tin_ref.at[1], tgt.at[3, 0, 1], 0, 1),
        send(tin_ref.at[1], tgt.at[1, 0, 1], 0, 3),
    ]
    own_head.wait()
    hboth[mine] = raw[0].T
    finish(first)
    second = [
        send(out_ref.at[0, 3, 0:q], out_ref.at[0, 2, 0:q], 1, 0),
        send(out_ref.at[0, 1, q:h], out_ref.at[0, 2, q:h], 3, 0),
        send(out_ref.at[3, 0, h:h + q], out_ref.at[2, 0, h:h + q], 0, 1),
        send(out_ref.at[1, 0, h + q:rows], out_ref.at[2, 0, h + q:rows], 0, 3),
        send(tgt.at[0, 3, 0], tgt.at[0, 2, 0], 1, 0),
        send(tgt.at[3, 0, 1], tgt.at[2, 0, 1], 0, 1),
    ]
    swap.wait()
    hboth[theirs] = raw[1].T
    finish(second)
    own.wait()
    sel.wait()
    third = [
        send(out_ref.at[0, :, 0:h], out_ref.at[3, :, 0:h], 0, 1),
        send(out_ref.at[0, :, 0:h], out_ref.at[1, :, 0:h], 0, 3),
        send(out_ref.at[:, 0, h:rows], out_ref.at[:, 3, h:rows], 1, 0),
        send(out_ref.at[:, 0, h:rows], out_ref.at[:, 1, h:rows], 3, 0),
        send(tgt.at[0, :, 0], tgt.at[3, :, 0], 0, 1),
        send(tgt.at[0, :, 0], tgt.at[1, :, 0], 0, 3),
        send(tgt.at[:, 0, 1], tgt.at[:, 3, 1], 1, 0),
        send(tgt.at[:, 0, 1], tgt.at[:, 1, 1], 3, 0),
    ]
    phase((0,))
    finish(third)
    fourth = [
        send(out_ref.at[3, :, 0:q], out_ref.at[2, :, 0:q], 0, 1),
        send(out_ref.at[1, :, q:h], out_ref.at[2, :, q:h], 0, 3),
        send(out_ref.at[:, 3, h:h + q], out_ref.at[:, 2, h:h + q], 1, 0),
        send(out_ref.at[:, 1, h + q:rows], out_ref.at[:, 2, h + q:rows], 3, 0),
        send(tgt.at[3, :, 0], tgt.at[2, :, 0], 0, 1),
        send(tgt.at[:, 3, 1], tgt.at[:, 2, 1], 1, 0),
    ]
    phase((1, 3))
    finish(fourth)
    phase((2,))


def gather_and_stats(piece, head_t, tin, n_tp):
    rows, cols = piece.shape
    vdev = head_t.shape[1]
    h = rows // 2
    return pl.pallas_call(
        functools.partial(fused_kernel, n_tp),
        out_shape=(
            jax.ShapeDtypeStruct((4, 4, rows, cols), piece.dtype),
            jax.ShapeDtypeStruct((8, 4, 4 * h), jnp.float32),
        ),
        in_specs=[pl.BlockSpec(memory_space=pl.ANY)] * 3,
        out_specs=(pl.BlockSpec(memory_space=pl.ANY), pl.BlockSpec(memory_space=pltpu.VMEM)),
        scratch_shapes=[
            pltpu.VMEM((2 * vdev, cols), jnp.bfloat16),
            pltpu.VMEM((2, cols, vdev), jnp.bfloat16),
            pltpu.VMEM((4, h, cols), jnp.bfloat16),
            pltpu.VMEM((4, 4, 2, 8, h), jnp.float32),
            pltpu.SemaphoreType.DMA((3,)),
            pltpu.SemaphoreType.DMA((2,)),
            pltpu.SemaphoreType.DMA((28,)),
            pltpu.SemaphoreType.DMA((28,)),
            pltpu.SemaphoreType.DMA((4,)),
        ],
        compiler_params=pltpu.CompilerParams(
            collective_id=1, has_side_effects=True, vmem_limit_bytes=60 * 1024 * 1024
        ),
    )(piece, head_t, tin)


def plane_kernel(n_tp, stats_ref, out_ref, own_sem, send_sems, recv_sems):
    xi, zi = lax.axis_index("x"), lax.axis_index("z")
    core, tp = lax.axis_index("core"), lax.axis_index("tp")
    offsets = [(dx, dz, dy) for dy in range(n_tp) for dz in range(4) for dx in range(4) if dx or dz or dy]

    def peer(dx, dz, dy):
        return (lax.rem(xi + dx, 4), lax.rem(zi + dz, 4), core, lax.rem(tp + dy, n_tp))

    barrier = pltpu.get_barrier_semaphore()
    for dx, dz, dy in offsets:
        pl.semaphore_signal(barrier, inc=1, device_id=peer(dx, dz, dy), device_id_type=MESH)
    pl.semaphore_wait(barrier, len(offsets))
    own = pltpu.make_async_copy(stats_ref.at[0, 0], out_ref.at[0, 0, 0], own_sem)
    own.start()
    cps = []
    for k, (dx, dz, dy) in enumerate(offsets):
        cp = pltpu.make_async_remote_copy(
            src_ref=stats_ref.at[dz, dx],
            dst_ref=out_ref.at[(n_tp - dy) % n_tp, (4 - dz) % 4, (4 - dx) % 4],
            send_sem=send_sems.at[k],
            recv_sem=recv_sems.at[k],
            device_id=peer(dx, dz, dy),
            device_id_type=MESH,
        )
        cp.start()
        cps.append(cp)
    own.wait()
    for cp in cps:
        cp.wait()


def exchange_all(stats, n_tp):
    n = n_tp * 16 - 1
    return pl.pallas_call(
        functools.partial(plane_kernel, n_tp),
        out_shape=jax.ShapeDtypeStruct((n_tp, *stats.shape), stats.dtype),
        in_specs=[pl.BlockSpec(memory_space=pl.ANY)],
        out_specs=pl.BlockSpec(memory_space=pl.ANY),
        scratch_shapes=[
            pltpu.SemaphoreType.DMA,
            pltpu.SemaphoreType.DMA((n,)),
            pltpu.SemaphoreType.DMA((n,)),
        ],
        compiler_params=pltpu.CompilerParams(collective_id=2, has_side_effects=True),
    )(stats)


def per_device(hidden_states, norm_gain, head, target_ids, lengths):
    feats = hidden_states.astype(jnp.float32)
    scale = lax.rsqrt(jnp.mean(feats * feats, axis=-1, keepdims=True) + 1e-06)
    normed = (feats * scale * norm_gain).astype(jnp.bfloat16)
    rows, dim = normed.shape
    vdev = head.shape[1]
    n_tp = lax.axis_size("tp")
    xi = lax.axis_index("x")
    zi = lax.axis_index("z")
    core = lax.axis_index("core")
    tp = lax.axis_index("tp")
    n_z = lax.axis_size("z")
    chip = xi * n_z + zi
    piece = normed
    head_t = head
    tin = jnp.broadcast_to(target_ids.astype(jnp.float32).reshape(2, 1, rows // 2), (2, 8, rows // 2))
    _, stats = gather_and_stats(piece, head_t, tin, n_tp)
    h = rows // 2
    st = stats.reshape(4, 2, 4, 4, h)
    by_offset = jnp.stack([st[0], st[3], st[2], st[1]])
    s_a = jnp.transpose(by_offset[:, 0], (1, 0, 2, 3))
    s_b = jnp.transpose(by_offset[:, 1], (1, 2, 0, 3))
    rel = jnp.concatenate([s_a, s_b], axis=3)
    arrived = exchange_all(jnp.moveaxis(rel, 0, 2), n_tp)
    arrived = jnp.roll(arrived, tp, axis=0)
    top, weight_sum, weighted, picked = merge(arrived.reshape(-1, 4, rows), axis=0)
    log_norm = top + jnp.log(weight_sum)
    live = jnp.arange(rows, dtype=jnp.int32) < lengths[0]
    logprob = jnp.where(live, picked - log_norm, jnp.float32(0.0))
    entropy = jnp.where(live, log_norm - weighted / weight_sum, jnp.float32(0.0))
    mean_lp = (jnp.sum(logprob) / lengths[0].astype(jnp.float32)).reshape(1)
    top_live = jnp.max(jnp.where(live, top, jnp.float32(-1e30))).reshape(1)
    return (logprob, entropy, mean_lp, top_live)


def solution(mesh):
    n_req, n_tp = mesh.devices.shape
    devices = np.asarray(mesh.devices).reshape(4, n_req // 8, 2, n_tp)
    fine = Mesh(devices, ("x", "z", "core", "tp"))
    rq = ("x", "z", "core")
    in_specs = (P(rq, None), P(), P(None, (*rq, "tp")), P(rq), P(rq))
    out_specs = (P(rq), P(rq), P(rq), P(rq))
    return jax.shard_map(
        per_device, mesh=fine, in_specs=in_specs, out_specs=out_specs, check_vma=False
    )
```

```python
import functools

import jax
import jax.numpy as jnp
import numpy as np
from jax import lax
from jax.experimental import pallas as pl
from jax.experimental.pallas import tpu as pltpu
from jax.sharding import Mesh, PartitionSpec as P

MESH = pl.DeviceIdType.MESH
EXTRA = 128


def slice_stats(block, target, matrix, vocab_ids):
    logits = jnp.dot(block, matrix, preferred_element_type=jnp.float32)
    top = jnp.max(logits, axis=-1)
    shifted = jnp.exp(logits - top[:, None])
    weight_sum = jnp.sum(shifted, axis=-1)
    weighted = jnp.sum(shifted * logits, axis=-1)
    hit = vocab_ids == target[:, None]
    picked = jnp.sum(jnp.where(hit, logits, 0.0), axis=-1)
    return jnp.stack([top, weight_sum, weighted, picked])


def merge(stats, axis):
    top = jnp.max(stats[:, 0], axis=axis)
    factor = jnp.exp(stats[:, 0] - jnp.expand_dims(top, axis))
    return (
        top,
        jnp.sum(stats[:, 1] * factor, axis=axis),
        jnp.sum(stats[:, 2] * factor, axis=axis),
        jnp.sum(stats[:, 3], axis=axis),
    )


def fused_kernel(n_tp, piece_ref, head_ref, tin_ref, out_ref, stats_ref,
                 hboth, raw, vbuf, tgt, local_sems, head_sems, send_sems, recv_sems, load_sems):
    xi, zi = lax.axis_index("x"), lax.axis_index("z")
    core, tp = lax.axis_index("core"), lax.axis_index("tp")
    vdev = head_ref.shape[1]

    def dev(dx, dz):
        return (lax.rem(xi + dx, 4), lax.rem(zi + dz, 4), core, tp)

    partner = (xi, zi, 1 - core, tp)
    barrier = pltpu.get_barrier_semaphore()
    for dx, dz in ((1, 0), (3, 0), (0, 1), (0, 3)):
        pl.semaphore_signal(barrier, inc=1, device_id=dev(dx, dz), device_id_type=MESH)
    pl.semaphore_signal(barrier, inc=1, device_id=partner, device_id_type=MESH)
    pl.semaphore_wait(barrier, 5)
    mine = pl.ds(pl.multiple_of(core * vdev, vdev), vdev)
    theirs = pl.ds(pl.multiple_of((1 - core) * vdev, vdev), vdev)
    swap = pltpu.make_async_remote_copy(
        src_ref=head_ref,
        dst_ref=raw.at[1],
        send_sem=head_sems.at[0],
        recv_sem=head_sems.at[1],
        device_id=partner,
        device_id_type=MESH,
    )
    swap.start()
    own_head = pltpu.make_async_copy(head_ref, raw.at[0], local_sems.at[0])
    own_head.start()
    sel = pltpu.make_async_copy(tin_ref, tgt.at[0, 0], local_sems.at[1])
    sel.start()
    own = pltpu.make_async_copy(piece_ref, out_ref.at[0, 0], local_sems.at[2])
    own.start()
    rows = piece_ref.shape[0]
    h, q = rows // 2, rows // 4
    count = [0]

    def send(src, dst, dx, dz):
        k = count[0]
        count[0] += 1
        cp = pltpu.make_async_remote_copy(
            src_ref=src,
            dst_ref=dst,
            send_sem=send_sems.at[k],
            recv_sem=recv_sems.at[k],
            device_id=dev(dx, dz),
            device_id_type=MESH,
        )
        cp.start()
        return cp

    def finish(cps):
        for cp in cps:
            cp.wait()

    chip = xi * 4 + zi
    ids = lax.broadcasted_iota(jnp.int32, (2 * vdev, 1), 0)
    vocab = (((chip * 2 + ids // vdev) * n_tp + tp) * vdev + ids % vdev).astype(jnp.float32)

    def group(m, half):
        off = lax.rem(m * 3, 4)
        loads = []
        for j in range(4):
            if half == 0:
                src = out_ref.at[off, j, pl.ds(0, h)]
            else:
                src = out_ref.at[j, off, pl.ds(h, h)]
            cp = pltpu.make_async_copy(src, vbuf.at[j], load_sems.at[j])
            cp.start()
            loads.append(cp)
        finish(loads)
        block = vbuf[...].reshape(4 * h, vbuf.shape[2])
        real = lax.dot_general(
            hboth[...], block, (((1,), (1,)), ((), ())), preferred_element_type=jnp.float32
        )
        if half == 0:
            pieces = [tgt[off, j, 0, 0:1, :] for j in range(4)]
        else:
            pieces = [tgt[j, off, 1, 0:1, :] for j in range(4)]
        target = jnp.concatenate(pieces, axis=1)
        top = jnp.max(real, axis=0, keepdims=True)
        shifted = jnp.exp(real - top)
        g = m * 2 + half
        stats_ref[g, 0:1, :] = top
        stats_ref[g, 1:2, :] = jnp.sum(shifted, axis=0, keepdims=True)
        stats_ref[g, 2:3, :] = jnp.sum(shifted * real, axis=0, keepdims=True)
        stats_ref[g, 3:4, :] = jnp.sum(jnp.where(vocab == target, real, 0.0), axis=0, keepdims=True)

    def phase(ms):
        def body(i, carry):
            m = ms[0] + i * (ms[1] - ms[0]) if len(ms) > 1 else ms[0] + i * 0
            group(m, 0)
            group(m, 1)
            return carry

        lax.fori_loop(0, len(ms), body, 0)

    first = [
        send(piece_ref.at[0:h], out_ref.at[0, 3, 0:h], 1, 0),
        send(piece_ref.at[0:h], out_ref.at[0, 1, 0:h], 3, 0),
        send(piece_ref.at[h:rows], out_ref.at[3, 0, h:rows], 0, 1),
        send(piece_ref.at[h:rows], out_ref.at[1, 0, h:rows], 0, 3),
        send(tin_ref.at[0], tgt.at[0, 3, 0], 1, 0),
        send(tin_ref.at[0], tgt.at[0, 1, 0], 3, 0),
        send(tin_ref.at[1], tgt.at[3, 0, 1], 0, 1),
        send(tin_ref.at[1], tgt.at[1, 0, 1], 0, 3),
    ]
    own_head.wait()
    hboth[mine] = raw[0].T
    finish(first)
    second = [
        send(out_ref.at[0, 3, 0:q], out_ref.at[0, 2, 0:q], 1, 0),
        send(out_ref.at[0, 1, q:h], out_ref.at[0, 2, q:h], 3, 0),
        send(out_ref.at[3, 0, h:h + q], out_ref.at[2, 0, h:h + q], 0, 1),
        send(out_ref.at[1, 0, h + q:rows], out_ref.at[2, 0, h + q:rows], 0, 3),
        send(tgt.at[0, 3, 0], tgt.at[0, 2, 0], 1, 0),
        send(tgt.at[3, 0, 1], tgt.at[2, 0, 1], 0, 1),
    ]
    swap.wait()
    hboth[theirs] = raw[1].T
    finish(second)
    own.wait()
    sel.wait()
    third = [
        send(out_ref.at[0, :, 0:h], out_ref.at[3, :, 0:h], 0, 1),
        send(out_ref.at[0, :, 0:h], out_ref.at[1, :, 0:h], 0, 3),
        send(out_ref.at[:, 0, h:rows], out_ref.at[:, 3, h:rows], 1, 0),
        send(out_ref.at[:, 0, h:rows], out_ref.at[:, 1, h:rows], 3, 0),
        send(tgt.at[0, :, 0], tgt.at[3, :, 0], 0, 1),
        send(tgt.at[0, :, 0], tgt.at[1, :, 0], 0, 3),
        send(tgt.at[:, 0, 1], tgt.at[:, 3, 1], 1, 0),
        send(tgt.at[:, 0, 1], tgt.at[:, 1, 1], 3, 0),
    ]
    phase((0,))
    finish(third)
    fourth = [
        send(out_ref.at[3, :, 0:q], out_ref.at[2, :, 0:q], 0, 1),
        send(out_ref.at[1, :, q:h], out_ref.at[2, :, q:h], 0, 3),
        send(out_ref.at[:, 3, h:h + q], out_ref.at[:, 2, h:h + q], 1, 0),
        send(out_ref.at[:, 1, h + q:rows], out_ref.at[:, 2, h + q:rows], 3, 0),
        send(tgt.at[3, :, 0], tgt.at[2, :, 0], 0, 1),
        send(tgt.at[:, 3, 1], tgt.at[:, 2, 1], 1, 0),
    ]
    phase((1, 3))
    finish(fourth)
    phase((2,))


def gather_and_stats(piece, head_t, tin, n_tp):
    rows, cols = piece.shape
    vdev = head_t.shape[1]
    h = rows // 2
    return pl.pallas_call(
        functools.partial(fused_kernel, n_tp),
        out_shape=(
            jax.ShapeDtypeStruct((4, 4, rows, cols), piece.dtype),
            jax.ShapeDtypeStruct((8, 4, 4 * h), jnp.float32),
        ),
        in_specs=[pl.BlockSpec(memory_space=pl.ANY)] * 3,
        out_specs=(pl.BlockSpec(memory_space=pl.ANY), pl.BlockSpec(memory_space=pltpu.VMEM)),
        scratch_shapes=[
            pltpu.VMEM((2 * vdev, cols), jnp.bfloat16),
            pltpu.VMEM((2, cols, vdev), jnp.bfloat16),
            pltpu.VMEM((4, h, cols), jnp.bfloat16),
            pltpu.VMEM((4, 4, 2, 8, h), jnp.float32),
            pltpu.SemaphoreType.DMA((3,)),
            pltpu.SemaphoreType.DMA((2,)),
            pltpu.SemaphoreType.DMA((28,)),
            pltpu.SemaphoreType.DMA((28,)),
            pltpu.SemaphoreType.DMA((4,)),
        ],
        compiler_params=pltpu.CompilerParams(
            collective_id=1, has_side_effects=True, vmem_limit_bytes=60 * 1024 * 1024
        ),
    )(piece, head_t, tin)


def plane_kernel(n_tp, stats_ref, out_ref, own_sem, send_sems, recv_sems):
    xi, zi = lax.axis_index("x"), lax.axis_index("z")
    core, tp = lax.axis_index("core"), lax.axis_index("tp")
    offsets = [(dx, dz, dy) for dy in range(n_tp) for dz in range(4) for dx in range(4) if dx or dz or dy]

    def peer(dx, dz, dy):
        return (lax.rem(xi + dx, 4), lax.rem(zi + dz, 4), core, lax.rem(tp + dy, n_tp))

    barrier = pltpu.get_barrier_semaphore()
    for dx, dz, dy in offsets:
        pl.semaphore_signal(barrier, inc=1, device_id=peer(dx, dz, dy), device_id_type=MESH)
    pl.semaphore_wait(barrier, len(offsets))
    own = pltpu.make_async_copy(stats_ref.at[0, 0], out_ref.at[0, 0, 0], own_sem)
    own.start()
    cps = []
    for k, (dx, dz, dy) in enumerate(offsets):
        cp = pltpu.make_async_remote_copy(
            src_ref=stats_ref.at[dz, dx],
            dst_ref=out_ref.at[(n_tp - dy) % n_tp, (4 - dz) % 4, (4 - dx) % 4],
            send_sem=send_sems.at[k],
            recv_sem=recv_sems.at[k],
            device_id=peer(dx, dz, dy),
            device_id_type=MESH,
        )
        cp.start()
        cps.append(cp)
    own.wait()
    for cp in cps:
        cp.wait()


def exchange_all(stats, n_tp):
    n = n_tp * 16 - 1
    return pl.pallas_call(
        functools.partial(plane_kernel, n_tp),
        out_shape=jax.ShapeDtypeStruct((n_tp, *stats.shape), stats.dtype),
        in_specs=[pl.BlockSpec(memory_space=pl.ANY)],
        out_specs=pl.BlockSpec(memory_space=pl.ANY),
        scratch_shapes=[
            pltpu.SemaphoreType.DMA,
            pltpu.SemaphoreType.DMA((n,)),
            pltpu.SemaphoreType.DMA((n,)),
        ],
        compiler_params=pltpu.CompilerParams(collective_id=2, has_side_effects=True),
    )(stats)


def norm_kernel(h_ref, g_ref, o_ref):
    feats = h_ref[...].astype(jnp.float32)
    scale = lax.rsqrt(jnp.mean(feats * feats, axis=-1, keepdims=True) + 1e-06)
    o_ref[...] = (feats * scale * g_ref[...]).astype(jnp.bfloat16)


def rms_norm(hidden_states, norm_gain):
    return pl.pallas_call(
        norm_kernel,
        out_shape=jax.ShapeDtypeStruct(hidden_states.shape, jnp.bfloat16),
    )(hidden_states, norm_gain.reshape(1, -1))


def per_device(hidden_states, norm_gain, head, target_ids, lengths):
    normed = rms_norm(hidden_states, norm_gain)
    rows, dim = normed.shape
    vdev = head.shape[1]
    n_tp = lax.axis_size("tp")
    xi = lax.axis_index("x")
    zi = lax.axis_index("z")
    core = lax.axis_index("core")
    tp = lax.axis_index("tp")
    n_z = lax.axis_size("z")
    chip = xi * n_z + zi
    piece = normed
    head_t = head
    tin = jnp.broadcast_to(target_ids.astype(jnp.float32).reshape(2, 1, rows // 2), (2, 8, rows // 2))
    _, stats = gather_and_stats(piece, head_t, tin, n_tp)
    h = rows // 2
    st = stats.reshape(4, 2, 4, 4, h)
    by_offset = jnp.stack([st[0], st[3], st[2], st[1]])
    s_a = jnp.transpose(by_offset[:, 0], (1, 0, 2, 3))
    s_b = jnp.transpose(by_offset[:, 1], (1, 2, 0, 3))
    rel = jnp.concatenate([s_a, s_b], axis=3)
    arrived = exchange_all(jnp.moveaxis(rel, 0, 2), n_tp)
    arrived = jnp.roll(arrived, tp, axis=0)
    top, weight_sum, weighted, picked = merge(arrived.reshape(-1, 4, rows), axis=0)
    log_norm = top + jnp.log(weight_sum)
    live = jnp.arange(rows, dtype=jnp.int32) < lengths[0]
    logprob = jnp.where(live, picked - log_norm, jnp.float32(0.0))
    entropy = jnp.where(live, log_norm - weighted / weight_sum, jnp.float32(0.0))
    mean_lp = (jnp.sum(logprob) / lengths[0].astype(jnp.float32)).reshape(1)
    top_live = jnp.max(jnp.where(live, top, jnp.float32(-1e30))).reshape(1)
    return (logprob, entropy, mean_lp, top_live)


def solution(mesh):
    n_req, n_tp = mesh.devices.shape
    devices = np.asarray(mesh.devices).reshape(4, n_req // 8, 2, n_tp)
    fine = Mesh(devices, ("x", "z", "core", "tp"))
    rq = ("x", "z", "core")
    in_specs = (P(rq, None), P(), P(None, (*rq, "tp")), P(rq), P(rq))
    out_specs = (P(rq), P(rq), P(rq), P(rq))
    return jax.shard_map(
        per_device, mesh=fine, in_specs=in_specs, out_specs=out_specs, check_vma=False
    )
```

```python
import functools

import jax
import jax.numpy as jnp
import numpy as np
from jax import lax
from jax.experimental import pallas as pl
from jax.experimental.pallas import tpu as pltpu
from jax.sharding import Mesh, PartitionSpec as P

MESH = pl.DeviceIdType.MESH
EXTRA = 128


def slice_stats(block, target, matrix, vocab_ids):
    logits = jnp.dot(block, matrix, preferred_element_type=jnp.float32)
    top = jnp.max(logits, axis=-1)
    shifted = jnp.exp(logits - top[:, None])
    weight_sum = jnp.sum(shifted, axis=-1)
    weighted = jnp.sum(shifted * logits, axis=-1)
    hit = vocab_ids == target[:, None]
    picked = jnp.sum(jnp.where(hit, logits, 0.0), axis=-1)
    return jnp.stack([top, weight_sum, weighted, picked])


def merge(stats, axis):
    top = jnp.max(stats[:, 0], axis=axis)
    factor = jnp.exp(stats[:, 0] - jnp.expand_dims(top, axis))
    return (
        top,
        jnp.sum(stats[:, 1] * factor, axis=axis),
        jnp.sum(stats[:, 2] * factor, axis=axis),
        jnp.sum(stats[:, 3], axis=axis),
    )


def fused_kernel(n_tp, piece_ref, head_ref, tin_ref, out_ref, stats_ref,
                 hboth, raw, vbuf, tgt, local_sems, head_sems, send_sems, recv_sems, load_sems):
    xi, zi = lax.axis_index("x"), lax.axis_index("z")
    core, tp = lax.axis_index("core"), lax.axis_index("tp")
    vdev = head_ref.shape[1]

    def dev(dx, dz):
        return (lax.rem(xi + dx, 4), lax.rem(zi + dz, 4), core, tp)

    partner = (xi, zi, 1 - core, tp)
    barrier = pltpu.get_barrier_semaphore()
    for dx, dz in ((1, 0), (3, 0), (0, 1), (0, 3)):
        pl.semaphore_signal(barrier, inc=1, device_id=dev(dx, dz), device_id_type=MESH)
    pl.semaphore_signal(barrier, inc=1, device_id=partner, device_id_type=MESH)
    pl.semaphore_wait(barrier, 5)
    mine = pl.ds(pl.multiple_of(core * vdev, vdev), vdev)
    theirs = pl.ds(pl.multiple_of((1 - core) * vdev, vdev), vdev)
    swap = pltpu.make_async_remote_copy(
        src_ref=head_ref,
        dst_ref=raw.at[1],
        send_sem=head_sems.at[0],
        recv_sem=head_sems.at[1],
        device_id=partner,
        device_id_type=MESH,
    )
    swap.start()
    own_head = pltpu.make_async_copy(head_ref, raw.at[0], local_sems.at[0])
    own_head.start()
    sel = pltpu.make_async_copy(tin_ref, tgt.at[0, 0], local_sems.at[1])
    sel.start()
    own = pltpu.make_async_copy(piece_ref, out_ref.at[0, 0], local_sems.at[2])
    own.start()
    rows = piece_ref.shape[0]
    h, q = rows // 2, rows // 4
    count = [0]

    def send(src, dst, dx, dz):
        k = count[0]
        count[0] += 1
        cp = pltpu.make_async_remote_copy(
            src_ref=src,
            dst_ref=dst,
            send_sem=send_sems.at[k],
            recv_sem=recv_sems.at[k],
            device_id=dev(dx, dz),
            device_id_type=MESH,
        )
        cp.start()
        return cp

    def finish(cps):
        for cp in cps:
            cp.wait()

    chip = xi * 4 + zi
    ids = lax.broadcasted_iota(jnp.int32, (2 * vdev, 1), 0)
    vocab = (((chip * 2 + ids // vdev) * n_tp + tp) * vdev + ids % vdev).astype(jnp.float32)

    def group(m, half):
        off = lax.rem(m * 3, 4)
        loads = []
        for j in range(4):
            if half == 0:
                src = out_ref.at[off, j, pl.ds(0, h)]
            else:
                src = out_ref.at[j, off, pl.ds(h, h)]
            cp = pltpu.make_async_copy(src, vbuf.at[j], load_sems.at[j])
            cp.start()
            loads.append(cp)
        finish(loads)
        block = vbuf[...].reshape(4 * h, vbuf.shape[2])
        real = lax.dot_general(
            hboth[...], block, (((1,), (1,)), ((), ())), preferred_element_type=jnp.float32
        )
        if half == 0:
            pieces = [tgt[off, j, 0, 0:1, :] for j in range(4)]
        else:
            pieces = [tgt[j, off, 1, 0:1, :] for j in range(4)]
        target = jnp.concatenate(pieces, axis=1).astype(jnp.float32)
        top = jnp.max(real, axis=0, keepdims=True)
        shifted = jnp.exp(real - top)
        g = m * 2 + half
        stats_ref[g, 0:1, :] = top
        stats_ref[g, 1:2, :] = jnp.sum(shifted, axis=0, keepdims=True)
        stats_ref[g, 2:3, :] = jnp.sum(shifted * real, axis=0, keepdims=True)
        stats_ref[g, 3:4, :] = jnp.sum(jnp.where(vocab == target, real, 0.0), axis=0, keepdims=True)

    def phase(ms):
        def body(i, carry):
            m = ms[0] + i * (ms[1] - ms[0]) if len(ms) > 1 else ms[0] + i * 0
            group(m, 0)
            group(m, 1)
            return carry

        lax.fori_loop(0, len(ms), body, 0)

    first = [
        send(piece_ref.at[0:h], out_ref.at[0, 3, 0:h], 1, 0),
        send(piece_ref.at[0:h], out_ref.at[0, 1, 0:h], 3, 0),
        send(piece_ref.at[h:rows], out_ref.at[3, 0, h:rows], 0, 1),
        send(piece_ref.at[h:rows], out_ref.at[1, 0, h:rows], 0, 3),
        send(tin_ref.at[0], tgt.at[0, 3, 0], 1, 0),
        send(tin_ref.at[0], tgt.at[0, 1, 0], 3, 0),
        send(tin_ref.at[1], tgt.at[3, 0, 1], 0, 1),
        send(tin_ref.at[1], tgt.at[1, 0, 1], 0, 3),
    ]
    own_head.wait()
    hboth[mine] = raw[0].T
    finish(first)
    second = [
        send(out_ref.at[0, 3, 0:q], out_ref.at[0, 2, 0:q], 1, 0),
        send(out_ref.at[0, 1, q:h], out_ref.at[0, 2, q:h], 3, 0),
        send(out_ref.at[3, 0, h:h + q], out_ref.at[2, 0, h:h + q], 0, 1),
        send(out_ref.at[1, 0, h + q:rows], out_ref.at[2, 0, h + q:rows], 0, 3),
        send(tgt.at[0, 3, 0], tgt.at[0, 2, 0], 1, 0),
        send(tgt.at[3, 0, 1], tgt.at[2, 0, 1], 0, 1),
    ]
    swap.wait()
    hboth[theirs] = raw[1].T
    finish(second)
    own.wait()
    sel.wait()
    third = [
        send(out_ref.at[0, :, 0:h], out_ref.at[3, :, 0:h], 0, 1),
        send(out_ref.at[0, :, 0:h], out_ref.at[1, :, 0:h], 0, 3),
        send(out_ref.at[:, 0, h:rows], out_ref.at[:, 3, h:rows], 1, 0),
        send(out_ref.at[:, 0, h:rows], out_ref.at[:, 1, h:rows], 3, 0),
        send(tgt.at[0, :, 0], tgt.at[3, :, 0], 0, 1),
        send(tgt.at[0, :, 0], tgt.at[1, :, 0], 0, 3),
        send(tgt.at[:, 0, 1], tgt.at[:, 3, 1], 1, 0),
        send(tgt.at[:, 0, 1], tgt.at[:, 1, 1], 3, 0),
    ]
    phase((0,))
    finish(third)
    fourth = [
        send(out_ref.at[3, :, 0:q], out_ref.at[2, :, 0:q], 0, 1),
        send(out_ref.at[1, :, q:h], out_ref.at[2, :, q:h], 0, 3),
        send(out_ref.at[:, 3, h:h + q], out_ref.at[:, 2, h:h + q], 1, 0),
        send(out_ref.at[:, 1, h + q:rows], out_ref.at[:, 2, h + q:rows], 3, 0),
        send(tgt.at[3, :, 0], tgt.at[2, :, 0], 0, 1),
        send(tgt.at[:, 3, 1], tgt.at[:, 2, 1], 1, 0),
    ]
    phase((1, 3))
    finish(fourth)
    phase((2,))


def gather_and_stats(piece, head_t, tin, n_tp):
    rows, cols = piece.shape
    vdev = head_t.shape[1]
    h = rows // 2
    return pl.pallas_call(
        functools.partial(fused_kernel, n_tp),
        out_shape=(
            jax.ShapeDtypeStruct((4, 4, rows, cols), piece.dtype),
            jax.ShapeDtypeStruct((8, 4, 4 * h), jnp.float32),
        ),
        in_specs=[pl.BlockSpec(memory_space=pl.ANY)] * 3,
        out_specs=(pl.BlockSpec(memory_space=pl.ANY), pl.BlockSpec(memory_space=pltpu.VMEM)),
        scratch_shapes=[
            pltpu.VMEM((2 * vdev, cols), jnp.bfloat16),
            pltpu.VMEM((2, cols, vdev), jnp.bfloat16),
            pltpu.VMEM((4, h, cols), jnp.bfloat16),
            pltpu.VMEM((4, 4, 2, 8, h), jnp.int32),
            pltpu.SemaphoreType.DMA((3,)),
            pltpu.SemaphoreType.DMA((2,)),
            pltpu.SemaphoreType.DMA((28,)),
            pltpu.SemaphoreType.DMA((28,)),
            pltpu.SemaphoreType.DMA((4,)),
        ],
        compiler_params=pltpu.CompilerParams(
            collective_id=1, has_side_effects=True, vmem_limit_bytes=60 * 1024 * 1024
        ),
    )(piece, head_t, tin)


def plane_kernel(n_tp, stats_ref, out_ref, own_sem, send_sems, recv_sems):
    xi, zi = lax.axis_index("x"), lax.axis_index("z")
    core, tp = lax.axis_index("core"), lax.axis_index("tp")
    offsets = [(dx, dz, dy) for dy in range(n_tp) for dz in range(4) for dx in range(4) if dx or dz or dy]

    def peer(dx, dz, dy):
        return (lax.rem(xi + dx, 4), lax.rem(zi + dz, 4), core, lax.rem(tp + dy, n_tp))

    barrier = pltpu.get_barrier_semaphore()
    for dx, dz, dy in offsets:
        pl.semaphore_signal(barrier, inc=1, device_id=peer(dx, dz, dy), device_id_type=MESH)
    pl.semaphore_wait(barrier, len(offsets))
    own = pltpu.make_async_copy(stats_ref.at[0, 0], out_ref.at[0, 0, 0], own_sem)
    own.start()
    cps = []
    for k, (dx, dz, dy) in enumerate(offsets):
        cp = pltpu.make_async_remote_copy(
            src_ref=stats_ref.at[dz, dx],
            dst_ref=out_ref.at[(n_tp - dy) % n_tp, (4 - dz) % 4, (4 - dx) % 4],
            send_sem=send_sems.at[k],
            recv_sem=recv_sems.at[k],
            device_id=peer(dx, dz, dy),
            device_id_type=MESH,
        )
        cp.start()
        cps.append(cp)
    own.wait()
    for cp in cps:
        cp.wait()


def exchange_all(stats, n_tp):
    n = n_tp * 16 - 1
    return pl.pallas_call(
        functools.partial(plane_kernel, n_tp),
        out_shape=jax.ShapeDtypeStruct((n_tp, *stats.shape), stats.dtype),
        in_specs=[pl.BlockSpec(memory_space=pl.ANY)],
        out_specs=pl.BlockSpec(memory_space=pl.ANY),
        scratch_shapes=[
            pltpu.SemaphoreType.DMA,
            pltpu.SemaphoreType.DMA((n,)),
            pltpu.SemaphoreType.DMA((n,)),
        ],
        compiler_params=pltpu.CompilerParams(collective_id=2, has_side_effects=True),
    )(stats)


def norm_kernel(h_ref, g_ref, o_ref):
    feats = h_ref[...].astype(jnp.float32)
    scale = lax.rsqrt(jnp.mean(feats * feats, axis=-1, keepdims=True) + 1e-06)
    o_ref[...] = (feats * scale * g_ref[...]).astype(jnp.bfloat16)


def rms_norm(hidden_states, norm_gain):
    return pl.pallas_call(
        norm_kernel,
        out_shape=jax.ShapeDtypeStruct(hidden_states.shape, jnp.bfloat16),
    )(hidden_states, norm_gain.reshape(1, -1))


def per_device(hidden_states, norm_gain, head, target_ids, lengths):
    normed = rms_norm(hidden_states, norm_gain)
    rows, dim = normed.shape
    vdev = head.shape[1]
    n_tp = lax.axis_size("tp")
    xi = lax.axis_index("x")
    zi = lax.axis_index("z")
    core = lax.axis_index("core")
    tp = lax.axis_index("tp")
    n_z = lax.axis_size("z")
    chip = xi * n_z + zi
    piece = normed
    head_t = head
    tin = jnp.broadcast_to(target_ids.reshape(2, 1, rows // 2), (2, 8, rows // 2))
    _, stats = gather_and_stats(piece, head_t, tin, n_tp)
    h = rows // 2
    st = stats.reshape(4, 2, 4, 4, h)
    by_offset = jnp.stack([st[0], st[3], st[2], st[1]])
    s_a = jnp.transpose(by_offset[:, 0], (1, 0, 2, 3))
    s_b = jnp.transpose(by_offset[:, 1], (1, 2, 0, 3))
    rel = jnp.concatenate([s_a, s_b], axis=3)
    arrived = exchange_all(jnp.moveaxis(rel, 0, 2), n_tp)
    arrived = jnp.roll(arrived, tp, axis=0)
    top, weight_sum, weighted, picked = merge(arrived.reshape(-1, 4, rows), axis=0)
    log_norm = top + jnp.log(weight_sum)
    live = jnp.arange(rows, dtype=jnp.int32) < lengths[0]
    logprob = jnp.where(live, picked - log_norm, jnp.float32(0.0))
    entropy = jnp.where(live, log_norm - weighted / weight_sum, jnp.float32(0.0))
    mean_lp = (jnp.sum(logprob) / lengths[0].astype(jnp.float32)).reshape(1)
    top_live = jnp.max(jnp.where(live, top, jnp.float32(-1e30))).reshape(1)
    return (logprob, entropy, mean_lp, top_live)


def solution(mesh):
    n_req, n_tp = mesh.devices.shape
    devices = np.asarray(mesh.devices).reshape(4, n_req // 8, 2, n_tp)
    fine = Mesh(devices, ("x", "z", "core", "tp"))
    rq = ("x", "z", "core")
    in_specs = (P(rq, None), P(), P(None, (*rq, "tp")), P(rq), P(rq))
    out_specs = (P(rq), P(rq), P(rq), P(rq))
    return jax.shard_map(
        per_device, mesh=fine, in_specs=in_specs, out_specs=out_specs, check_vma=False
    )
```
